32 devices in a mesh: groups: 2 (over x), aa: 8 (over z, y), ba: 2 (over core).
Axes of the slice: x: 2, y: 2, z: 4, core: 2. Of those that a mesh axis runs over, the one named last changes fastest.
Arguments:
- video: bfloat16 [128, 8, 32, 512], P('groups', 'aa', 'ba'), parts along dimension 0, may hold values from -6 to 6
- norm_gain: float32 [3, 512], replicated, may hold values from 0.1 to 1.9
- qkv_weight: bfloat16 [3, 512, 1536], replicated, may hold values from -8 to 8
- out_weight: bfloat16 [3, 512, 512], replicated, may hold values from -0.25 to 0.25
Outputs:
- result: bfloat16 [128, 8, 32, 512], P('groups', 'aa', 'ba'), parts along dimension 0
The draws below stay inside these ranges and needn't reach their ends.
There are 2 independent parts, one for each index of `groups`. The reference program is written for one: setup_inputs(seed, part) draws one part's arguments, and reference() takes and returns one part's arrays. A program takes and returns all parts, laid end to end along the dimension named above; an argument that names none is the same for every part. Nothing has to cross between parts.
All inputs are finite; a program needn't handle non-finite values.
Results may differ from the reference program's by a relative error of at most 0.014.
Values may be sent and summed in bfloat16 or wider, within the bound.
No kernel may reach another device: no remote copies, remote signals or barrier semaphores. Data moves between devices by JAX's collectives and lax.ppermute only.
A program may use at most 64 MiB of HBM per device.

```python
import math
import jax
import jax.numpy as jnp
from jax import lax

D = 512
HEADS = 8
HEAD_DIM = 64
BLOCKS = 3
FRAMES = 64
WIDTH = 32
HEIGHT = 8


def draw_qkv_weight(key, part):
    first_key = jax.random.fold_in(key, 0)
    drawn = jnp.clip(jax.random.normal(first_key, (BLOCKS, D, 3 * D), jnp.float32), -6.0, 6.0) * (1.0 / math.sqrt(D))
    return jnp.clip(drawn, -8.0, 8.0).astype(jnp.bfloat16)


def shard_levels(stream_key, shape, shards, smallest, largest):
    factor_of = 1.0
    for position, shards_of in shards:
        heights = jax.random.uniform(jax.random.fold_in(jax.random.fold_in(stream_key, 6), position), (shards_of,), jnp.float32, smallest / len(shards), largest / len(shards))
        factor_of = factor_of * jnp.repeat(jnp.exp(heights), shape[position] // shards_of).reshape((-1,) + (1,) * (len(shape) - 1 - position))
    return factor_of


def bell_draw(rng, dims, scale, most, cuts=(), dtype=jnp.bfloat16):
    array = scale * jax.random.normal(rng, dims, jnp.float32)
    if cuts:
        array = array * shard_levels(rng, dims, cuts, -0.22, 0.18)
    return jnp.clip(array, -most, most).astype(dtype)


def setup_inputs(seed: int = 0, part: int = 0) -> dict:
    key_list = jax.random.split(jax.random.key(seed), 5)
    part_keys = jax.random.split(jax.random.fold_in(key_list[4], part), 5)
    return {
        "video": bell_draw(part_keys[0], (FRAMES, HEIGHT, WIDTH, D), 1.0, 6.0, ((1, 8), (2, 2))),
        "norm_gain": jnp.clip(1.0 + 0.18 * jax.random.normal(key_list[1], (BLOCKS, D), jnp.float32), 0.1, 1.9),
        "qkv_weight": draw_qkv_weight(jax.random.fold_in(key_list[4], 71), part),
        "out_weight": bell_draw(key_list[3], (BLOCKS, D, D), D ** -0.5, 0.25),
    }


score_forms = ('sbcnd,tbcnd->bcnst', 'ascnd,atcnd->acnst', 'absnd,abtnd->abnst')
mix_forms = ('bcnst,tbcnd->sbcnd', 'acnst,atcnd->ascnd', 'abnst,abtnd->absnd')

def attend(queries, key_rows, value_rows, line):
    shape = queries.shape
    split = shape[:3] + (HEADS, HEAD_DIM)
    scores = jnp.einsum(score_forms[line], queries.reshape(split).astype(jnp.float32), key_rows.reshape(split).astype(jnp.float32)) * (1.0 / math.sqrt(HEAD_DIM))
    weights = jax.nn.softmax(scores, axis=-1).astype(jnp.bfloat16)
    mixed = jnp.einsum(mix_forms[line], weights.astype(jnp.float32), value_rows.reshape(split).astype(jnp.float32))
    return mixed.astype(jnp.bfloat16).reshape(shape)

def full_block(state, gain, weight_in, weight_out, line):
    floats = state.astype(jnp.float32)
    meansq = lax.optimization_barrier(jnp.mean(floats * floats, axis=-1, keepdims=True))
    normed = (floats * lax.rsqrt(meansq + 1e-06) * gain).astype(jnp.bfloat16)
    packed = jnp.dot(normed, weight_in, preferred_element_type=jnp.float32).astype(jnp.bfloat16)
    width = state.shape[-1]
    mixed = attend(packed[..., :width], packed[..., width:2 * width], packed[..., 2 * width:], line)
    update = jnp.dot(mixed, weight_out, preferred_element_type=jnp.float32)
    return (floats + update).astype(jnp.bfloat16)

def reference(video, norm_gain, qkv_weight, out_weight):
    by_row = jnp.moveaxis(video, 1, 0)
    by_row = lax.map(lambda plane: full_block(plane[None], norm_gain[0], qkv_weight[0], out_weight[0], 1)[0], by_row)
    state = jnp.moveaxis(by_row, 0, 1)
    state = lax.map(lambda plane: full_block(plane[None], norm_gain[1], qkv_weight[1], out_weight[1], 1)[0], state)
    state = lax.map(lambda plane: full_block(plane[None], norm_gain[2], qkv_weight[2], out_weight[2], 2)[0], state)
    return state
```

```python
import functools
import math

import jax
import jax.numpy as jnp
from jax import lax
from jax.experimental import pallas as pl
from jax.experimental.pallas import tpu as pltpu
from jax.sharding import PartitionSpec as P

HEADS = 8
HEAD_DIM = 64
EPS = 1e-06
LANES = 128
HIDDEN = -1e30


score_forms = ("sbcnd,tbcnd->bcnst", "ascnd,atcnd->acnst", "absnd,abtnd->abnst")
mix_forms = ("bcnst,tbcnd->sbcnd", "acnst,atcnd->ascnd", "abnst,abtnd->absnd")


def attend(queries, key_rows, value_rows, line):
    shape = queries.shape
    split = shape[:3] + (HEADS, HEAD_DIM)
    scores = jnp.einsum(
        score_forms[line],
        queries.reshape(split),
        key_rows.reshape(split),
        preferred_element_type=jnp.float32,
    ) * (1.0 / math.sqrt(HEAD_DIM))
    weights = jax.nn.softmax(scores, axis=-1).astype(jnp.bfloat16)
    mixed = jnp.einsum(
        mix_forms[line], weights, value_rows.reshape(split), preferred_element_type=jnp.float32
    )
    return mixed.astype(jnp.bfloat16).reshape(shape)


def full_block(state, gain, weight_in, weight_out, line):
    floats = state.astype(jnp.float32)
    meansq = jnp.mean(floats * floats, axis=-1, keepdims=True)
    normed = (floats * lax.rsqrt(meansq + EPS) * gain).astype(jnp.bfloat16)
    packed = jnp.dot(normed, weight_in, preferred_element_type=jnp.float32).astype(jnp.bfloat16)
    width = state.shape[-1]
    mixed = attend(
        packed[..., :width], packed[..., width : 2 * width], packed[..., 2 * width :], line
    )
    update = jnp.dot(mixed, weight_out, preferred_element_type=jnp.float32)
    return (floats + update).astype(jnp.bfloat16)


def general_body(video, norm_gain, qkv_weight, out_weight):
    state = full_block(video, norm_gain[0], qkv_weight[0], out_weight[0], 0)
    state = lax.all_to_all(state, "aa", split_axis=0, concat_axis=1, tiled=True)
    state = full_block(state, norm_gain[1], qkv_weight[1], out_weight[1], 1)
    state = lax.all_to_all(state, "ba", split_axis=1, concat_axis=2, tiled=True)
    state = full_block(state, norm_gain[2], qkv_weight[2], out_weight[2], 2)
    state = lax.all_to_all(state, "ba", split_axis=2, concat_axis=1, tiled=True)
    return lax.all_to_all(state, "aa", split_axis=1, concat_axis=0, tiled=True)


def normalise(floats, gain):
    meansq = jnp.mean(floats * floats, axis=-1, keepdims=True)
    return (floats * lax.rsqrt(meansq + EPS) * gain).astype(jnp.bfloat16)


def tile_attention(packed, same_line):
    tokens, width = packed.shape[0], packed.shape[1] // 3
    left = lax.broadcasted_iota(jnp.int32, (tokens, LANES), 1) < HEAD_DIM
    left_half = left.astype(jnp.bfloat16)
    right_half = (1 - left.astype(jnp.float32)).astype(jnp.bfloat16)
    ones = jnp.ones((tokens, LANES), jnp.bfloat16)
    scale = math.log2(math.e) / math.sqrt(HEAD_DIM)
    pieces = []
    for pair in range(width // LANES):
        at = pair * LANES
        q = packed[:, at : at + LANES]
        k = packed[:, width + at : width + at + LANES]
        v = packed[:, 2 * width + at : 2 * width + at + LANES]
        both = jnp.concatenate([q * left_half, q * right_half], axis=0)
        scores = lax.dot_general(
            both, k, (((1,), (1,)), ((), ())), preferred_element_type=jnp.float32
        )
        scores = jnp.where(
            same_line[None], scores.reshape(2, tokens, tokens), HIDDEN
        ).reshape(2 * tokens, tokens)
        top = jnp.max(scores, axis=-1, keepdims=True)
        weights = jnp.exp2((scores - top) * scale).astype(jnp.bfloat16)
        mixed = jnp.dot(
            weights, jnp.concatenate([v, ones], axis=1), preferred_element_type=jnp.float32
        )
        mixed = mixed[:, :LANES] / mixed[:, LANES:]
        pieces.append(jnp.where(left, mixed[:tokens], mixed[tokens:]).astype(jnp.bfloat16))
    return jnp.concatenate(pieces, axis=1)


def line_mask(tokens, line_of):
    rows = lax.broadcasted_iota(jnp.int32, (tokens, tokens), 0)
    columns = lax.broadcasted_iota(jnp.int32, (tokens, tokens), 1)
    return line_of(rows) == line_of(columns)


def project(normed_ref, weight_ref, packed_ref, rows=256):
    total = normed_ref.shape[0]
    rows = min(rows, total)
    for at in range(0, total, rows):
        packed_ref[at : at + rows] = jnp.dot(
            normed_ref[at : at + rows], weight_ref[...], preferred_element_type=jnp.float32
        ).astype(jnp.bfloat16)


def first_kernel(
    block, me_ref, x_ref, gain_ref, win_hbm, wout_hbm, *rest
):
    n = len(rest) - 8
    outs = rest[:n]
    win, wout, natural, lined, normed, packed, mixed, sems = rest[n:]
    frames, columns, width = x_ref.shape
    tokens = frames * columns
    copy_in = pltpu.make_async_copy(win_hbm.at[block], win, sems.at[0])
    copy_out = pltpu.make_async_copy(wout_hbm.at[block], wout, sems.at[1])
    copy_in.start()
    copy_out.start()
    floats = x_ref[...].reshape(tokens, width).astype(jnp.float32)
    for at in range(width // LANES):
        natural[at] = floats[:, at * LANES : (at + 1) * LANES]
    gain = gain_ref[block : block + 1]
    for column in range(columns):
        piece = jnp.concatenate(
            [natural[at, pl.ds(column, frames, stride=columns), :] for at in range(width // LANES)],
            axis=1,
        )
        lined[column * frames : (column + 1) * frames] = piece
        normed[column * frames : (column + 1) * frames] = normalise(piece, gain)
    copy_in.wait()
    project(normed, win, packed)
    tile = LANES if LANES % frames == 0 else frames
    mask = line_mask(tile, lambda i: i // frames)

    def attend_tile(step, carry):
        rows = pl.ds(pl.multiple_of(step * tile, tile), tile)
        mixed[rows] = tile_attention(packed[rows], mask)
        return carry

    lax.fori_loop(0, tokens // tile, attend_tile, 0)
    copy_out.wait()
    for at in range(0, tokens, 256):
        lined[at : at + 256] += jnp.dot(
            mixed[at : at + 256], wout[...], preferred_element_type=jnp.float32
        )
    piece = frames // n
    for k in range(n):
        start = jnp.bitwise_xor(me_ref[0], k) * piece
        for column in range(columns):
            rows = pl.ds(pl.multiple_of(column * frames + start, piece), piece)
            outs[k][column] = lined[rows].astype(jnp.bfloat16)


def middle_kernel(block, core_ref, *rest):
    n = len(rest) - 13
    ins = rest[:n]
    gain_ref, win_hbm, wout_hbm, keep_ref, give_ref = rest[n : n + 5]
    win, wout, lined, normed, packed, mixed, sems, _ = rest[n + 5 :]
    columns, frames, width = ins[0].shape
    per = columns * frames
    tokens = n * per
    copy_in = pltpu.make_async_copy(win_hbm.at[block], win, sems.at[0])
    copy_out = pltpu.make_async_copy(wout_hbm.at[block], wout, sems.at[1])
    copy_in.start()
    copy_out.start()
    gain = gain_ref[block : block + 1]
    for k in range(n):
        floats = ins[k][...].reshape(per, width).astype(jnp.float32)
        lined[k * per : (k + 1) * per] = floats
        normed[k * per : (k + 1) * per] = normalise(floats, gain)
    copy_in.wait()
    project(normed, win, packed)
    share = LANES // n
    mask = line_mask(LANES, lambda i: i % share)

    def attend_tile(step, carry):
        at = pl.multiple_of(step * share, share)
        piece = jnp.concatenate(
            [packed[pl.ds(pl.multiple_of(k * per + at, share), share)] for k in range(n)], axis=0
        )
        result = tile_attention(piece, mask)
        for k in range(n):
            mixed[pl.ds(pl.multiple_of(k * per + at, share), share)] = result[
                k * share : (k + 1) * share
            ]
        return carry

    lax.fori_loop(0, per // share, attend_tile, 0)
    copy_out.wait()
    for at in range(0, tokens, 256):
        lined[at : at + 256] += jnp.dot(
            mixed[at : at + 256], wout[...], preferred_element_type=jnp.float32
        )
    core = core_ref[0]
    for half in range(n // 2):
        mine = pl.ds(pl.multiple_of((2 * half + core) * per, per), per)
        other = pl.ds(pl.multiple_of((2 * half + 1 - core) * per, per), per)
        keep_ref[half] = lined[mine].astype(jnp.bfloat16).reshape(columns, frames, width)
        give_ref[half] = lined[other].astype(jnp.bfloat16).reshape(columns, frames, width)


def last_kernel(block, keep_ref, got_ref, gain_ref, win_hbm, wout_hbm, *rest):
    count = keep_ref.shape[0]
    outs = rest[: 2 * count]
    win, wout, lined, normed, packed, mixed, sems, final = rest[2 * count :]
    _, columns, frames, width = keep_ref.shape
    per = columns * frames
    copy_in = pltpu.make_async_copy(win_hbm.at[block], win, sems.at[0])
    copy_out = pltpu.make_async_copy(wout_hbm.at[block], wout, sems.at[1])
    copy_in.start()
    copy_out.start()
    gain = gain_ref[block : block + 1]
    for row in range(count):
        for half, ref in enumerate((keep_ref, got_ref)):
            at = (2 * row + half) * per
            floats = ref[row].reshape(per, width).astype(jnp.float32)
            lined[at : at + per] = floats
            normed[at : at + per] = normalise(floats, gain)
    copy_in.wait()
    project(normed, win, packed)
    tile = 2 * per
    mask = line_mask(tile, lambda i: i % frames)

    def attend_tile(step, carry):
        rows = pl.ds(pl.multiple_of(step * tile, tile), tile)
        mixed[rows] = tile_attention(packed[rows], mask)
        return carry

    lax.fori_loop(0, count, attend_tile, 0)
    copy_out.wait()
    for row in range(count):
        at = row * tile
        result = lined[at : at + tile] + jnp.dot(
            mixed[at : at + tile], wout[...], preferred_element_type=jnp.float32
        )
        for lane in range(width // LANES):
            final[lane, at : at + tile] = result[:, lane * LANES : (lane + 1) * LANES]
    for row in range(count):
        for half in range(2):
            for frame in range(frames):
                start = (2 * row + half) * per + frame
                outs[2 * row + half][frame] = jnp.concatenate(
                    [
                        final[lane, pl.ds(start, columns, stride=frames), :].astype(jnp.bfloat16)
                        for lane in range(width // LANES)
                    ],
                    axis=1,
                )


def join_kernel(starts_ref, *rest):
    pieces, out, sems = rest[:-2], rest[-2], rest[-1]
    size = pieces[0].shape[0]
    copies = []
    for index, piece in enumerate(pieces):
        where = pl.ds(starts_ref[index] * size, size)
        copies.append(pltpu.make_async_copy(piece, out.at[where], sems.at[index]))
        copies[-1].start()
    for copy in copies:
        copy.wait()


SMEM = pl.BlockSpec(memory_space=pltpu.SMEM)
VMEM = pl.BlockSpec(memory_space=pltpu.VMEM)
ANY = pl.BlockSpec(memory_space=pl.ANY)


def scratch(tokens, width):
    return [
        pltpu.VMEM((width, 3 * width), jnp.bfloat16),
        pltpu.VMEM((width, width), jnp.bfloat16),
        pltpu.VMEM((tokens, width), jnp.float32),
        pltpu.VMEM((tokens, width), jnp.bfloat16),
        pltpu.VMEM((tokens, 3 * width), jnp.bfloat16),
        pltpu.VMEM((tokens, width), jnp.bfloat16),
        pltpu.SemaphoreType.DMA((2,)),
    ]


PARAMS = dict(compiler_params=pltpu.CompilerParams(vmem_limit_bytes=48 << 20))


def fast_body(n, video, norm_gain, qkv_weight, out_weight):
    frames, _, columns, width = video.shape
    piece = frames // n
    tokens = frames * columns
    spot = lax.axis_index("aa")
    core = lax.axis_index("ba")
    bf16 = jnp.bfloat16
    message = jax.ShapeDtypeStruct((columns, piece, width), bf16)
    weights = (norm_gain, qkv_weight, out_weight)

    sent = pl.pallas_call(
        functools.partial(first_kernel, 0),
        out_shape=[message] * n,
        in_specs=[SMEM, VMEM, VMEM, ANY, ANY],
        out_specs=[VMEM] * n,
        scratch_shapes=scratch(tokens, width)[:2]
        + [pltpu.VMEM((width // LANES, tokens, LANES), jnp.float32)]
        + scratch(tokens, width)[2:],
        name="first",
        **PARAMS,
    )(spot[None], video.reshape(frames, columns, width), *weights)

    order = list(range(n - 1, 0, -1))
    came = {0: sent[0]}
    for k in order:
        came[k] = lax.ppermute(sent[k], "aa", [(i, i ^ k) for i in range(n)])

    half = jax.ShapeDtypeStruct((n // 2, columns, piece, width), bf16)
    keep, give = pl.pallas_call(
        functools.partial(middle_kernel, 1),
        out_shape=[half, half],
        in_specs=[SMEM] + [VMEM] * n + [VMEM, ANY, ANY],
        out_specs=[VMEM] * 2,
        scratch_shapes=scratch(tokens, width) + [pltpu.SMEM((1,), jnp.int32)],
        name="middle",
        **PARAMS,
    )(core[None], *[came[k] for k in range(n)], *weights)

    got = lax.ppermute(give, "ba", [(0, 1), (1, 0)])

    home = jax.ShapeDtypeStruct((piece, columns, width), bf16)
    results = pl.pallas_call(
        functools.partial(last_kernel, 2),
        out_shape=[home] * n,
        in_specs=[VMEM, VMEM, VMEM, ANY, ANY],
        out_specs=[VMEM] * n,
        scratch_shapes=scratch(tokens, width)
        + [pltpu.VMEM((width // LANES, tokens, LANES), jnp.float32)],
        name="last",
        **PARAMS,
    )(keep, got, *weights)

    arrived, starts = [], []
    for index in order + [0]:
        row, swap = index // 2, index % 2
        pairs = [
            (2 * a + b, 2 * (a ^ (2 * row + b)) + (b ^ swap)) for a in range(n) for b in range(2)
        ]
        arrived.append(lax.ppermute(results[index], ("aa", "ba"), pairs))
        starts.append(jnp.bitwise_xor(spot, 2 * row + jnp.bitwise_xor(core, swap)))

    out = pl.pallas_call(
        join_kernel,
        out_shape=jax.ShapeDtypeStruct((frames, columns, width), bf16),
        in_specs=[SMEM] + [ANY] * n,
        out_specs=ANY,
        scratch_shapes=[pltpu.SemaphoreType.DMA((n,))],
        name="join",
    )(jnp.stack(starts).astype(jnp.int32), *arrived)
    return out.reshape(video.shape)


def body(n, cores, video, norm_gain, qkv_weight, out_weight):
    frames, rows, columns, width = video.shape
    piece = frames // n
    fast = (
        cores == 2
        and rows == 1
        and n % 2 == 0
        and n & (n - 1) == 0
        and LANES % n == 0
        and piece % 8 == 0
        and LANES % frames == 0
        and (LANES // n) % 16 == 0
        and columns % 16 == 0
        and (columns * piece) % (LANES // n) == 0
        and width % LANES == 0
        and width == HEADS * HEAD_DIM
        and (frames * columns) % 256 == 0
    )
    if fast:
        return fast_body(n, video, norm_gain, qkv_weight, out_weight)
    return general_body(video, norm_gain, qkv_weight, out_weight)


def solution(mesh):
    return jax.shard_map(
        functools.partial(body, mesh.shape["aa"], mesh.shape["ba"]),
        mesh=mesh,
        in_specs=(P("groups", "aa", "ba", None), P(), P(), P()),
        out_specs=P("groups", "aa", "ba", None),
        check_vma=False,
    )
```

```python
import functools
import math

import jax
import jax.numpy as jnp
from jax import lax
from jax.experimental import pallas as pl
from jax.experimental.pallas import tpu as pltpu
from jax.sharding import PartitionSpec as P

HEADS = 8
HEAD_DIM = 64
EPS = 1e-06
LANES = 128
HIDDEN = -1e30


score_forms = ("sbcnd,tbcnd->bcnst", "ascnd,atcnd->acnst", "absnd,abtnd->abnst")
mix_forms = ("bcnst,tbcnd->sbcnd", "acnst,atcnd->ascnd", "abnst,abtnd->absnd")


def attend(queries, key_rows, value_rows, line):
    shape = queries.shape
    split = shape[:3] + (HEADS, HEAD_DIM)
    scores = jnp.einsum(
        score_forms[line],
        queries.reshape(split),
        key_rows.reshape(split),
        preferred_element_type=jnp.float32,
    ) * (1.0 / math.sqrt(HEAD_DIM))
    weights = jax.nn.softmax(scores, axis=-1).astype(jnp.bfloat16)
    mixed = jnp.einsum(
        mix_forms[line], weights, value_rows.reshape(split), preferred_element_type=jnp.float32
    )
    return mixed.astype(jnp.bfloat16).reshape(shape)


def full_block(state, gain, weight_in, weight_out, line):
    floats = state.astype(jnp.float32)
    meansq = jnp.mean(floats * floats, axis=-1, keepdims=True)
    normed = (floats * lax.rsqrt(meansq + EPS) * gain).astype(jnp.bfloat16)
    packed = jnp.dot(normed, weight_in, preferred_element_type=jnp.float32).astype(jnp.bfloat16)
    width = state.shape[-1]
    mixed = attend(
        packed[..., :width], packed[..., width : 2 * width], packed[..., 2 * width :], line
    )
    update = jnp.dot(mixed, weight_out, preferred_element_type=jnp.float32)
    return (floats + update).astype(jnp.bfloat16)


def general_body(video, norm_gain, qkv_weight, out_weight):
    state = full_block(video, norm_gain[0], qkv_weight[0], out_weight[0], 0)
    state = lax.all_to_all(state, "aa", split_axis=0, concat_axis=1, tiled=True)
    state = full_block(state, norm_gain[1], qkv_weight[1], out_weight[1], 1)
    state = lax.all_to_all(state, "ba", split_axis=1, concat_axis=2, tiled=True)
    state = full_block(state, norm_gain[2], qkv_weight[2], out_weight[2], 2)
    state = lax.all_to_all(state, "ba", split_axis=2, concat_axis=1, tiled=True)
    return lax.all_to_all(state, "aa", split_axis=1, concat_axis=0, tiled=True)


def normalise(floats, gain):
    meansq = jnp.mean(floats * floats, axis=-1, keepdims=True)
    return (floats * lax.rsqrt(meansq + EPS) * gain).astype(jnp.bfloat16)


def tile_attention(packed, same_line):
    tokens, width = packed.shape[0], packed.shape[1] // 3
    left = lax.broadcasted_iota(jnp.int32, (tokens, LANES), 1) < HEAD_DIM
    left_half = left.astype(jnp.bfloat16)
    right_half = (1 - left.astype(jnp.float32)).astype(jnp.bfloat16)
    ones = jnp.ones((tokens, LANES), jnp.bfloat16)
    scale = math.log2(math.e) / math.sqrt(HEAD_DIM)
    pieces = []
    for pair in range(width // LANES):
        at = pair * LANES
        q = packed[:, at : at + LANES]
        k = packed[:, width + at : width + at + LANES]
        v = packed[:, 2 * width + at : 2 * width + at + LANES]
        both = jnp.concatenate([q * left_half, q * right_half], axis=0)
        scores = lax.dot_general(
            both, k, (((1,), (1,)), ((), ())), preferred_element_type=jnp.float32
        )
        scores = jnp.where(
            same_line[None], scores.reshape(2, tokens, tokens), HIDDEN
        ).reshape(2 * tokens, tokens)
        top = jnp.max(scores, axis=-1, keepdims=True)
        weights = jnp.exp2((scores - top) * scale).astype(jnp.bfloat16)
        mixed = jnp.dot(
            weights, jnp.concatenate([v, ones], axis=1), preferred_element_type=jnp.float32
        )
        mixed = mixed[:, :LANES] / mixed[:, LANES:]
        pieces.append(jnp.where(left, mixed[:tokens], mixed[tokens:]).astype(jnp.bfloat16))
    return jnp.concatenate(pieces, axis=1)


def line_mask(tokens, line_of):
    rows = lax.broadcasted_iota(jnp.int32, (tokens, tokens), 0)
    columns = lax.broadcasted_iota(jnp.int32, (tokens, tokens), 1)
    return line_of(rows) == line_of(columns)


def project(normed_ref, weight_ref, packed_ref, rows=256):
    total = normed_ref.shape[0]
    rows = min(rows, total)
    for at in range(0, total, rows):
        packed_ref[at : at + rows] = jnp.dot(
            normed_ref[at : at + rows], weight_ref[...], preferred_element_type=jnp.float32
        ).astype(jnp.bfloat16)


def first_kernel(
    block, me_ref, x_hbm, gain_hbm, win_hbm, wout_hbm, *rest
):
    n = len(rest) - 10
    outs = rest[:n]
    win, wout, natural, lined, normed, packed, mixed, sems, x_ref, gain_ref = rest[n:]
    frames, columns, width = x_ref.shape
    tokens = frames * columns
    copy_x = pltpu.make_async_copy(x_hbm, x_ref, sems.at[2])
    copy_gain = pltpu.make_async_copy(gain_hbm, gain_ref, sems.at[3])
    copy_x.start()
    copy_gain.start()
    copy_in = pltpu.make_async_copy(win_hbm.at[block], win, sems.at[0])
    copy_out = pltpu.make_async_copy(wout_hbm.at[block], wout, sems.at[1])
    copy_in.start()
    copy_out.start()
    copy_x.wait()
    copy_gain.wait()
    floats = x_ref[...].reshape(tokens, width).astype(jnp.float32)
    for at in range(width // LANES):
        natural[at] = floats[:, at * LANES : (at + 1) * LANES]
    gain = gain_ref[block : block + 1]
    for column in range(columns):
        piece = jnp.concatenate(
            [natural[at, pl.ds(column, frames, stride=columns), :] for at in range(width // LANES)],
            axis=1,
        )
        lined[column * frames : (column + 1) * frames] = piece
        normed[column * frames : (column + 1) * frames] = normalise(piece, gain)
    copy_in.wait()
    project(normed, win, packed)
    tile = LANES if LANES % frames == 0 else frames
    mask = line_mask(tile, lambda i: i // frames)

    def attend_tile(step, carry):
        rows = pl.ds(pl.multiple_of(step * tile, tile), tile)
        mixed[rows] = tile_attention(packed[rows], mask)
        return carry

    lax.fori_loop(0, tokens // tile, attend_tile, 0)
    copy_out.wait()
    for at in range(0, tokens, 256):
        lined[at : at + 256] += jnp.dot(
            mixed[at : at + 256], wout[...], preferred_element_type=jnp.float32
        )
    piece = frames // n
    for k in range(n):
        start = jnp.bitwise_xor(me_ref[0], k) * piece
        for column in range(columns):
            rows = pl.ds(pl.multiple_of(column * frames + start, piece), piece)
            outs[k][column] = lined[rows].astype(jnp.bfloat16)


def middle_kernel(block, core_ref, *rest):
    n = len(rest) - 13
    ins = rest[:n]
    gain_hbm, win_hbm, wout_hbm, keep_ref, give_ref = rest[n : n + 5]
    win, wout, lined, normed, packed, mixed, sems, gain_ref = rest[n + 5 :]
    copy_gain = pltpu.make_async_copy(gain_hbm, gain_ref, sems.at[3])
    copy_gain.start()
    columns, frames, width = ins[0].shape
    per = columns * frames
    tokens = n * per
    copy_in = pltpu.make_async_copy(win_hbm.at[block], win, sems.at[0])
    copy_out = pltpu.make_async_copy(wout_hbm.at[block], wout, sems.at[1])
    copy_in.start()
    copy_out.start()
    copy_gain.wait()
    gain = gain_ref[block : block + 1]
    for k in range(n):
        floats = ins[k][...].reshape(per, width).astype(jnp.float32)
        lined[k * per : (k + 1) * per] = floats
        normed[k * per : (k + 1) * per] = normalise(floats, gain)
    copy_in.wait()
    project(normed, win, packed)
    share = LANES // n
    mask = line_mask(LANES, lambda i: i % share)

    def attend_tile(step, carry):
        at = pl.multiple_of(step * share, share)
        piece = jnp.concatenate(
            [packed[pl.ds(pl.multiple_of(k * per + at, share), share)] for k in range(n)], axis=0
        )
        result = tile_attention(piece, mask)
        for k in range(n):
            mixed[pl.ds(pl.multiple_of(k * per + at, share), share)] = result[
                k * share : (k + 1) * share
            ]
        return carry

    lax.fori_loop(0, per // share, attend_tile, 0)
    copy_out.wait()
    for at in range(0, tokens, 256):
        lined[at : at + 256] += jnp.dot(
            mixed[at : at + 256], wout[...], preferred_element_type=jnp.float32
        )
    core = core_ref[0]
    for half in range(n // 2):
        mine = pl.ds(pl.multiple_of((2 * half + core) * per, per), per)
        other = pl.ds(pl.multiple_of((2 * half + 1 - core) * per, per), per)
        keep_ref[half] = lined[mine].astype(jnp.bfloat16).reshape(columns, frames, width)
        give_ref[half] = lined[other].astype(jnp.bfloat16).reshape(columns, frames, width)


def last_kernel(block, keep_ref, got_ref, gain_hbm, win_hbm, wout_hbm, *rest):
    count = keep_ref.shape[0]
    outs = rest[: 2 * count]
    win, wout, lined, normed, packed, mixed, sems, gain_ref, final = rest[2 * count :]
    copy_gain = pltpu.make_async_copy(gain_hbm, gain_ref, sems.at[3])
    copy_gain.start()
    _, columns, frames, width = keep_ref.shape
    per = columns * frames
    copy_in = pltpu.make_async_copy(win_hbm.at[block], win, sems.at[0])
    copy_out = pltpu.make_async_copy(wout_hbm.at[block], wout, sems.at[1])
    copy_in.start()
    copy_out.start()
    copy_gain.wait()
    gain = gain_ref[block : block + 1]
    for row in range(count):
        for half, ref in enumerate((keep_ref, got_ref)):
            at = (2 * row + half) * per
            floats = ref[row].reshape(per, width).astype(jnp.float32)
            lined[at : at + per] = floats
            normed[at : at + per] = normalise(floats, gain)
    copy_in.wait()
    project(normed, win, packed)
    tile = 2 * per
    mask = line_mask(tile, lambda i: i % frames)

    def attend_tile(step, carry):
        rows = pl.ds(pl.multiple_of(step * tile, tile), tile)
        mixed[rows] = tile_attention(packed[rows], mask)
        return carry

    lax.fori_loop(0, count, attend_tile, 0)
    copy_out.wait()
    for row in range(count):
        at = row * tile
        result = lined[at : at + tile] + jnp.dot(
            mixed[at : at + tile], wout[...], preferred_element_type=jnp.float32
        )
        for lane in range(width // LANES):
            final[lane, at : at + tile] = result[:, lane * LANES : (lane + 1) * LANES]
    for row in range(count):
        for half in range(2):
            for frame in range(frames):
                start = (2 * row + half) * per + frame
                outs[2 * row + half][frame] = jnp.concatenate(
                    [
                        final[lane, pl.ds(start, columns, stride=frames), :].astype(jnp.bfloat16)
                        for lane in range(width // LANES)
                    ],
                    axis=1,
                )


def join_kernel(starts_ref, *rest):
    pieces, out, sems = rest[:-2], rest[-2], rest[-1]
    size = pieces[0].shape[0]
    copies = []
    for index, piece in enumerate(pieces):
        where = pl.ds(starts_ref[index] * size, size)
        copies.append(pltpu.make_async_copy(piece, out.at[where], sems.at[index]))
        copies[-1].start()
    for copy in copies:
        copy.wait()


SMEM = pl.BlockSpec(memory_space=pltpu.SMEM)
VMEM = pl.BlockSpec(memory_space=pltpu.VMEM)
HBM = pl.BlockSpec(memory_space=pltpu.HBM)


def scratch(tokens, width):
    return [
        pltpu.VMEM((width, 3 * width), jnp.bfloat16),
        pltpu.VMEM((width, width), jnp.bfloat16),
        pltpu.VMEM((tokens, width), jnp.float32),
        pltpu.VMEM((tokens, width), jnp.bfloat16),
        pltpu.VMEM((tokens, 3 * width), jnp.bfloat16),
        pltpu.VMEM((tokens, width), jnp.bfloat16),
        pltpu.SemaphoreType.DMA((4,)),
    ]


PARAMS = dict(compiler_params=pltpu.CompilerParams(vmem_limit_bytes=48 << 20))


def fast_body(n, video, norm_gain, qkv_weight, out_weight):
    frames, _, columns, width = video.shape
    piece = frames // n
    tokens = frames * columns
    spot = lax.axis_index("aa")
    core = lax.axis_index("ba")
    bf16 = jnp.bfloat16
    message = jax.ShapeDtypeStruct((columns, piece, width), bf16)
    local = pltpu.with_memory_space_constraint(
        video.reshape(frames, columns, width), pltpu.HBM
    )
    weights = tuple(
        pltpu.with_memory_space_constraint(w, pltpu.HBM)
        for w in (norm_gain, qkv_weight, out_weight)
    )

    sent = pl.pallas_call(
        functools.partial(first_kernel, 0),
        out_shape=[message] * n,
        in_specs=[SMEM, HBM, HBM, HBM, HBM],
        out_specs=[VMEM] * n,
        scratch_shapes=scratch(tokens, width)[:2]
        + [pltpu.VMEM((width // LANES, tokens, LANES), jnp.float32)]
        + scratch(tokens, width)[2:]
        + [
            pltpu.VMEM((frames, columns, width), bf16),
            pltpu.VMEM(norm_gain.shape, jnp.float32),
        ],
        name="first",
        **PARAMS,
    )(spot[None], local, *weights)

    order = list(range(n - 1, 0, -1))
    came = {0: sent[0]}
    for k in order:
        came[k] = lax.ppermute(sent[k], "aa", [(i, i ^ k) for i in range(n)])

    half = jax.ShapeDtypeStruct((n // 2, columns, piece, width), bf16)
    keep, give = pl.pallas_call(
        functools.partial(middle_kernel, 1),
        out_shape=[half, half],
        in_specs=[SMEM] + [VMEM] * n + [HBM, HBM, HBM],
        out_specs=[VMEM] * 2,
        scratch_shapes=scratch(tokens, width) + [pltpu.VMEM(norm_gain.shape, jnp.float32)],
        name="middle",
        **PARAMS,
    )(core[None], *[came[k] for k in range(n)], *weights)

    got = lax.ppermute(give, "ba", [(0, 1), (1, 0)])

    home = jax.ShapeDtypeStruct((piece, columns, width), bf16)
    results = pl.pallas_call(
        functools.partial(last_kernel, 2),
        out_shape=[home] * n,
        in_specs=[VMEM, VMEM, HBM, HBM, HBM],
        out_specs=[VMEM] * n,
        scratch_shapes=scratch(tokens, width)
        + [
            pltpu.VMEM(norm_gain.shape, jnp.float32),
            pltpu.VMEM((width // LANES, tokens, LANES), jnp.float32),
        ],
        name="last",
        **PARAMS,
    )(keep, got, *weights)

    arrived, starts = [], []
    for index in order + [0]:
        row, swap = index // 2, index % 2
        pairs = [
            (2 * a + b, 2 * (a ^ (2 * row + b)) + (b ^ swap)) for a in range(n) for b in range(2)
        ]
        arrived.append(lax.ppermute(results[index], ("aa", "ba"), pairs))
        starts.append(jnp.bitwise_xor(spot, 2 * row + jnp.bitwise_xor(core, swap)))

    out = pl.pallas_call(
        join_kernel,
        out_shape=jax.ShapeDtypeStruct((frames, columns, width), bf16),
        in_specs=[SMEM] + [VMEM] * n,
        out_specs=HBM,
        scratch_shapes=[pltpu.SemaphoreType.DMA((n,))],
        name="join",
        compiler_params=pltpu.CompilerParams(vmem_limit_bytes=4 << 20),
    )(jnp.stack(starts).astype(jnp.int32), *arrived)
    return out.reshape(video.shape)


def body(n, cores, video, norm_gain, qkv_weight, out_weight):
    frames, rows, columns, width = video.shape
    piece = frames // n
    fast = (
        cores == 2
        and rows == 1
        and n % 2 == 0
        and n & (n - 1) == 0
        and LANES % n == 0
        and piece % 8 == 0
        and LANES % frames == 0
        and (LANES // n) % 16 == 0
        and columns % 16 == 0
        and (columns * piece) % (LANES // n) == 0
        and width % LANES == 0
        and width == HEADS * HEAD_DIM
        and (frames * columns) % 256 == 0
    )
    if fast:
        return fast_body(n, video, norm_gain, qkv_weight, out_weight)
    return general_body(video, norm_gain, qkv_weight, out_weight)


def solution(mesh):
    return jax.shard_map(
        functools.partial(body, mesh.shape["aa"], mesh.shape["ba"]),
        mesh=mesh,
        in_specs=(P("groups", "aa", "ba", None), P(), P(), P()),
        out_specs=P("groups", "aa", "ba", None),
        check_vma=False,
    )
```

```python
import functools
import math

import jax
import jax.numpy as jnp
from jax import lax
from jax.experimental import pallas as pl
from jax.experimental.pallas import tpu as pltpu
from jax.sharding import PartitionSpec as P

HEADS = 8
HEAD_DIM = 64
EPS = 1e-06
LANES = 128
HIDDEN = -1e30


score_forms = ("sbcnd,tbcnd->bcnst", "ascnd,atcnd->acnst", "absnd,abtnd->abnst")
mix_forms = ("bcnst,tbcnd->sbcnd", "acnst,atcnd->ascnd", "abnst,abtnd->absnd")


def attend(queries, key_rows, value_rows, line):
    shape = queries.shape
    split = shape[:3] + (HEADS, HEAD_DIM)
    scores = jnp.einsum(
        score_forms[line],
        queries.reshape(split),
        key_rows.reshape(split),
        preferred_element_type=jnp.float32,
    ) * (1.0 / math.sqrt(HEAD_DIM))
    weights = jax.nn.softmax(scores, axis=-1).astype(jnp.bfloat16)
    mixed = jnp.einsum(
        mix_forms[line], weights, value_rows.reshape(split), preferred_element_type=jnp.float32
    )
    return mixed.astype(jnp.bfloat16).reshape(shape)


def full_block(state, gain, weight_in, weight_out, line):
    floats = state.astype(jnp.float32)
    meansq = jnp.mean(floats * floats, axis=-1, keepdims=True)
    normed = (floats * lax.rsqrt(meansq + EPS) * gain).astype(jnp.bfloat16)
    packed = jnp.dot(normed, weight_in, preferred_element_type=jnp.float32).astype(jnp.bfloat16)
    width = state.shape[-1]
    mixed = attend(
        packed[..., :width], packed[..., width : 2 * width], packed[..., 2 * width :], line
    )
    update = jnp.dot(mixed, weight_out, preferred_element_type=jnp.float32)
    return (floats + update).astype(jnp.bfloat16)


def general_body(video, norm_gain, qkv_weight, out_weight):
    state = full_block(video, norm_gain[0], qkv_weight[0], out_weight[0], 0)
    state = lax.all_to_all(state, "aa", split_axis=0, concat_axis=1, tiled=True)
    state = full_block(state, norm_gain[1], qkv_weight[1], out_weight[1], 1)
    state = lax.all_to_all(state, "ba", split_axis=1, concat_axis=2, tiled=True)
    state = full_block(state, norm_gain[2], qkv_weight[2], out_weight[2], 2)
    state = lax.all_to_all(state, "ba", split_axis=2, concat_axis=1, tiled=True)
    return lax.all_to_all(state, "aa", split_axis=1, concat_axis=0, tiled=True)


def normalise(floats, gain):
    meansq = jnp.mean(floats * floats, axis=-1, keepdims=True)
    return (floats * lax.rsqrt(meansq + EPS) * gain).astype(jnp.bfloat16)


def lane_halves(tokens):
    left = lax.broadcasted_iota(jnp.int32, (tokens, LANES), 1) < HEAD_DIM
    left = left.astype(jnp.float32)
    return left.astype(jnp.bfloat16), (1 - left).astype(jnp.bfloat16)


def tile_attention(packed, same_line, halves):
    tokens, width = packed.shape[0], packed.shape[1] // 3
    left, right = halves
    pieces = []
    for at in range(0, width, LANES):
        q = packed[:, at : at + LANES]
        k = packed[:, width + at : width + at + LANES]
        v = packed[:, 2 * width + at : 2 * width + at + LANES]
        scores = lax.dot_general(
            q,
            jnp.concatenate([k * left, k * right], axis=0),
            (((1,), (1,)), ((), ())),
            preferred_element_type=jnp.float32,
        )
        weights = []
        for head in range(2):
            own = jnp.where(same_line, scores[:, head * tokens : (head + 1) * tokens], HIDDEN)
            top = jnp.max(own, axis=-1, keepdims=True)
            weights.append(jnp.exp2(own - top).astype(jnp.bfloat16))
        values = jnp.concatenate(
            [
                jnp.concatenate([v * left, left], axis=1),
                jnp.concatenate([v * right, right], axis=1),
            ],
            axis=0,
        )
        mixed = jnp.dot(
            jnp.concatenate(weights, axis=1), values, preferred_element_type=jnp.float32
        )
        pieces.append((mixed[:, :LANES] / mixed[:, LANES:]).astype(jnp.bfloat16))
    return jnp.concatenate(pieces, axis=1)


def line_mask(tokens, line_of):
    rows = lax.broadcasted_iota(jnp.int32, (tokens, tokens), 0)
    columns = lax.broadcasted_iota(jnp.int32, (tokens, tokens), 1)
    return line_of(rows) == line_of(columns)


def project(normed, weight_ref, packed_ref, at):
    rows, width = normed.shape
    result = jnp.dot(normed, weight_ref[...], preferred_element_type=jnp.float32)
    scale = math.log2(math.e) / math.sqrt(HEAD_DIM)
    packed_ref[at : at + rows, :width] = (result[:, :width] * scale).astype(jnp.bfloat16)
    packed_ref[at : at + rows, width:] = result[:, width:].astype(jnp.bfloat16)


def lanes_of(value):
    return [value[:, at : at + LANES] for at in range(0, value.shape[1], LANES)]


def strided(ref, start, size, stride):
    return jnp.concatenate(
        [ref[at, pl.ds(start, size, stride=stride), :] for at in range(ref.shape[0])], axis=1
    )


def first_kernel(block, me_ref, x_hbm, gain_hbm, win_hbm, wout_hbm, *rest):
    n = len(rest) - 9
    outs = rest[:n]
    win, wout, natural, lined, packed, mixed, sems, x_ref, gain_ref = rest[n:]
    frames, columns, width = x_ref.shape
    tokens = frames * columns
    loads = [
        pltpu.make_async_copy(source, target, sems.at[index])
        for index, (source, target) in enumerate(
            (
                (x_hbm, x_ref),
                (gain_hbm, gain_ref),
                (win_hbm.at[block], win),
                (wout_hbm.at[block], wout),
            )
        )
    ]
    for load in loads:
        load.start()
    loads[0].wait()
    loads[1].wait()
    for at, lanes in enumerate(lanes_of(x_ref[...].reshape(tokens, width).astype(jnp.float32))):
        natural[at] = lanes
    gain = gain_ref[block : block + 1]
    group = 256 // frames
    for column in range(0, columns, group):
        pieces = []
        for each in range(column, column + group):
            floats = strided(natural, each, frames, columns)
            for at, lanes in enumerate(lanes_of(floats)):
                lined[at, each * frames : (each + 1) * frames] = lanes
            pieces.append(normalise(floats, gain))
        if column == 0:
            loads[2].wait()
        project(jnp.concatenate(pieces, axis=0), win, packed, column * frames)
    mask = line_mask(LANES, lambda i: i // frames)
    halves = lane_halves(LANES)
    for at in range(0, tokens, LANES):
        mixed[at : at + LANES] = tile_attention(packed[at : at + LANES], mask, halves)
    loads[3].wait()
    for at in range(0, tokens, 256):
        update = jnp.dot(mixed[at : at + 256], wout[...], preferred_element_type=jnp.float32)
        for index, lanes in enumerate(lanes_of(update)):
            lined[index, at : at + 256] += lanes
    piece = frames // n
    for k in range(n):
        start = jnp.bitwise_xor(me_ref[0], k) * piece
        for frame in range(piece):
            outs[k][frame] = strided(lined, start + frame, columns, frames).astype(jnp.bfloat16)


def middle_kernel(block, core_ref, *rest):
    n = len(rest) - 12
    ins = rest[:n]
    gain_hbm, win_hbm, wout_hbm, keep_ref, give_ref = rest[n : n + 5]
    win, wout, lined, packed, mixed, sems, gain_ref = rest[n + 5 :]
    frames, columns, width = ins[0].shape
    per = columns * frames
    tokens = n * per
    loads = [
        pltpu.make_async_copy(source, target, sems.at[index])
        for index, (source, target) in enumerate(
            ((gain_hbm, gain_ref), (win_hbm.at[block], win), (wout_hbm.at[block], wout))
        )
    ]
    for load in loads:
        load.start()
    loads[0].wait()
    gain = gain_ref[block : block + 1]
    for k in range(0, n, 2):
        pieces = []
        for each in (k, k + 1):
            floats = ins[each][...].reshape(per, width).astype(jnp.float32)
            lined[each * per : (each + 1) * per] = floats
            pieces.append(normalise(floats, gain))
        if k == 0:
            loads[1].wait()
        project(jnp.concatenate(pieces, axis=0), win, packed, k * per)
    share = LANES // n
    mask = line_mask(LANES, lambda i: i % share)
    halves = lane_halves(LANES)
    for at in range(0, per, share):
        tile = jnp.concatenate(
            [packed[k * per + at : k * per + at + share] for k in range(n)], axis=0
        )
        result = tile_attention(tile, mask, halves)
        for k in range(n):
            mixed[k * per + at : k * per + at + share] = result[k * share : (k + 1) * share]
    loads[2].wait()
    for at in range(0, tokens, 256):
        lined[at : at + 256] += jnp.dot(
            mixed[at : at + 256], wout[...], preferred_element_type=jnp.float32
        )
    core = core_ref[0]
    for half in range(n // 2):
        mine = pl.ds(pl.multiple_of((2 * half + core) * per, per), per)
        other = pl.ds(pl.multiple_of((2 * half + 1 - core) * per, per), per)
        keep_ref[half] = lined[mine].astype(jnp.bfloat16).reshape(frames, columns, width)
        give_ref[half] = lined[other].astype(jnp.bfloat16).reshape(frames, columns, width)


def last_kernel(block, keep_ref, got_ref, gain_hbm, win_hbm, wout_hbm, *rest):
    count = keep_ref.shape[0]
    outs = rest[: 2 * count]
    win, wout, lined, packed, mixed, sems, gain_ref = rest[2 * count :]
    _, frames, columns, width = keep_ref.shape
    tile = 2 * frames * columns
    loads = [
        pltpu.make_async_copy(source, target, sems.at[index])
        for index, (source, target) in enumerate(
            ((gain_hbm, gain_ref), (win_hbm.at[block], win), (wout_hbm.at[block], wout))
        )
    ]
    for load in loads:
        load.start()
    loads[0].wait()
    gain = gain_ref[block : block + 1]
    for row in range(count):
        both = jnp.concatenate([keep_ref[row], got_ref[row]], axis=1)
        floats = both.reshape(tile, width).astype(jnp.float32)
        lined[row * tile : (row + 1) * tile] = floats
        normed = normalise(floats, gain)
        if row == 0:
            loads[1].wait()
        project(normed, win, packed, row * tile)
    mask = line_mask(LANES, lambda i: i // (2 * columns))
    halves = lane_halves(LANES)
    for at in range(0, count * tile, LANES):
        mixed[at : at + LANES] = tile_attention(packed[at : at + LANES], mask, halves)
    loads[2].wait()
    for row in range(count):
        at = row * tile
        result = lined[at : at + tile] + jnp.dot(
            mixed[at : at + tile], wout[...], preferred_element_type=jnp.float32
        )
        result = result.astype(jnp.bfloat16).reshape(frames, 2 * columns, width)
        outs[2 * row][...] = result[:, :columns]
        outs[2 * row + 1][...] = result[:, columns:]


def join_kernel(starts_ref, *rest):
    pieces, out, sems = rest[:-2], rest[-2], rest[-1]
    size = pieces[0].shape[0]
    copies = []
    for index, piece in enumerate(pieces):
        where = pl.ds(starts_ref[index] * size, size)
        copies.append(pltpu.make_async_copy(piece, out.at[where], sems.at[index]))
        copies[-1].start()
    for copy in copies:
        copy.wait()


SMEM = pl.BlockSpec(memory_space=pltpu.SMEM)
VMEM = pl.BlockSpec(memory_space=pltpu.VMEM)
HBM = pl.BlockSpec(memory_space=pltpu.HBM)


def scratch(tokens, width):
    return [
        pltpu.VMEM((width, 3 * width), jnp.bfloat16),
        pltpu.VMEM((width, width), jnp.bfloat16),
        pltpu.VMEM((tokens, width), jnp.float32),
        pltpu.VMEM((tokens, 3 * width), jnp.bfloat16),
        pltpu.VMEM((tokens, width), jnp.bfloat16),
        pltpu.SemaphoreType.DMA((4,)),
    ]


PARAMS = dict(compiler_params=pltpu.CompilerParams(vmem_limit_bytes=48 << 20))


def fast_body(n, video, norm_gain, qkv_weight, out_weight):
    frames, _, columns, width = video.shape
    piece = frames // n
    tokens = frames * columns
    spot = lax.axis_index("aa")
    core = lax.axis_index("ba")
    bf16 = jnp.bfloat16
    message = jax.ShapeDtypeStruct((piece, columns, width), bf16)
    local = pltpu.with_memory_space_constraint(
        video.reshape(frames, columns, width), pltpu.HBM
    )
    weights = tuple(
        pltpu.with_memory_space_constraint(w, pltpu.HBM)
        for w in (norm_gain, qkv_weight, out_weight)
    )

    sent = pl.pallas_call(
        functools.partial(first_kernel, 0),
        out_shape=[message] * n,
        in_specs=[SMEM, HBM, HBM, HBM, HBM],
        out_specs=[VMEM] * n,
        scratch_shapes=scratch(tokens, width)[:2]
        + [pltpu.VMEM((width // LANES, tokens, LANES), jnp.float32)] * 2
        + scratch(tokens, width)[3:]
        + [
            pltpu.VMEM((frames, columns, width), bf16),
            pltpu.VMEM(norm_gain.shape, jnp.float32),
        ],
        name="first",
        **PARAMS,
    )(spot[None], local, *weights)

    order = list(range(n - 1, 0, -1))
    came = {0: sent[0]}
    for k in order:
        came[k] = lax.ppermute(sent[k], "aa", [(i, i ^ k) for i in range(n)])

    half = jax.ShapeDtypeStruct((n // 2, piece, columns, width), bf16)
    keep, give = pl.pallas_call(
        functools.partial(middle_kernel, 1),
        out_shape=[half, half],
        in_specs=[SMEM] + [VMEM] * n + [HBM, HBM, HBM],
        out_specs=[VMEM] * 2,
        scratch_shapes=scratch(tokens, width) + [pltpu.VMEM(norm_gain.shape, jnp.float32)],
        name="middle",
        **PARAMS,
    )(core[None], *[came[k] for k in range(n)], *weights)

    got = lax.ppermute(give, "ba", [(0, 1), (1, 0)])

    results = pl.pallas_call(
        functools.partial(last_kernel, 2),
        out_shape=[message] * n,
        in_specs=[VMEM, VMEM, HBM, HBM, HBM],
        out_specs=[VMEM] * n,
        scratch_shapes=scratch(tokens, width)
        + [pltpu.VMEM(norm_gain.shape, jnp.float32)],
        name="last",
        **PARAMS,
    )(keep, got, *weights)

    arrived, starts = [], []
    for index in order + [0]:
        row, swap = index // 2, index % 2
        pairs = [
            (2 * a + b, 2 * (a ^ (2 * row + b)) + (b ^ swap)) for a in range(n) for b in range(2)
        ]
        arrived.append(lax.ppermute(results[index], ("aa", "ba"), pairs))
        starts.append(jnp.bitwise_xor(spot, 2 * row + jnp.bitwise_xor(core, swap)))

    out = pl.pallas_call(
        join_kernel,
        out_shape=jax.ShapeDtypeStruct((frames, columns, width), bf16),
        in_specs=[SMEM] + [VMEM] * n,
        out_specs=HBM,
        scratch_shapes=[pltpu.SemaphoreType.DMA((n,))],
        name="join",
        compiler_params=pltpu.CompilerParams(vmem_limit_bytes=4 << 20),
    )(jnp.stack(starts).astype(jnp.int32), *arrived)
    return out.reshape(video.shape)


def body(n, cores, video, norm_gain, qkv_weight, out_weight):
    frames, rows, columns, width = video.shape
    piece = frames // n
    fast = (
        cores == 2
        and rows == 1
        and n % 2 == 0
        and n & (n - 1) == 0
        and LANES % n == 0
        and (LANES // n) % 16 == 0
        and frames % n == 0
        and LANES % frames == 0
        and frames % 8 == 0
        and columns % 16 == 0
        and LANES % (2 * columns) == 0
        and (columns * piece) % LANES == 0
        and (frames * columns) % 256 == 0
        and width == HEADS * HEAD_DIM
        and width % LANES == 0
    )
    if fast:
        return fast_body(n, video, norm_gain, qkv_weight, out_weight)
    return general_body(video, norm_gain, qkv_weight, out_weight)


def solution(mesh):
    return jax.shard_map(
        functools.partial(body, mesh.shape["aa"], mesh.shape["ba"]),
        mesh=mesh,
        in_specs=(P("groups", "aa", "ba", None), P(), P(), P()),
        out_specs=P("groups", "aa", "ba", None),
        check_vma=False,
    )
```

```python
import functools
import math

import jax
import jax.numpy as jnp
from jax import lax
from jax.experimental import pallas as pl
from jax.experimental.pallas import tpu as pltpu
from jax.sharding import PartitionSpec as P

HEADS = 8
HEAD_DIM = 64
EPS = 1e-06
LANES = 128
HIDDEN = -1e30
FIRST_ORDER = (4, 1, 5, 2, 6, 3, 7)
LAST_ROWS = ((2,), (3,), (1, 0))


score_forms = ("sbcnd,tbcnd->bcnst", "ascnd,atcnd->acnst", "absnd,abtnd->abnst")
mix_forms = ("bcnst,tbcnd->sbcnd", "acnst,atcnd->ascnd", "abnst,abtnd->absnd")


def attend(queries, key_rows, value_rows, line):
    shape = queries.shape
    split = shape[:3] + (HEADS, HEAD_DIM)
    scores = jnp.einsum(
        score_forms[line],
        queries.reshape(split),
        key_rows.reshape(split),
        preferred_element_type=jnp.float32,
    ) * (1.0 / math.sqrt(HEAD_DIM))
    weights = jax.nn.softmax(scores, axis=-1).astype(jnp.bfloat16)
    mixed = jnp.einsum(
        mix_forms[line], weights, value_rows.reshape(split), preferred_element_type=jnp.float32
    )
    return mixed.astype(jnp.bfloat16).reshape(shape)


def full_block(state, gain, weight_in, weight_out, line):
    floats = state.astype(jnp.float32)
    meansq = jnp.mean(floats * floats, axis=-1, keepdims=True)
    normed = (floats * lax.rsqrt(meansq + EPS) * gain).astype(jnp.bfloat16)
    packed = jnp.dot(normed, weight_in, preferred_element_type=jnp.float32).astype(jnp.bfloat16)
    width = state.shape[-1]
    mixed = attend(
        packed[..., :width], packed[..., width : 2 * width], packed[..., 2 * width :], line
    )
    update = jnp.dot(mixed, weight_out, preferred_element_type=jnp.float32)
    return (floats + update).astype(jnp.bfloat16)


def general_body(video, norm_gain, qkv_weight, out_weight):
    state = full_block(video, norm_gain[0], qkv_weight[0], out_weight[0], 0)
    state = lax.all_to_all(state, "aa", split_axis=0, concat_axis=1, tiled=True)
    state = full_block(state, norm_gain[1], qkv_weight[1], out_weight[1], 1)
    state = lax.all_to_all(state, "ba", split_axis=1, concat_axis=2, tiled=True)
    state = full_block(state, norm_gain[2], qkv_weight[2], out_weight[2], 2)
    state = lax.all_to_all(state, "ba", split_axis=2, concat_axis=1, tiled=True)
    return lax.all_to_all(state, "aa", split_axis=1, concat_axis=0, tiled=True)


def normalise(floats, gain):
    meansq = jnp.mean(floats * floats, axis=-1, keepdims=True)
    return (floats * lax.rsqrt(meansq + EPS) * gain).astype(jnp.bfloat16)


def lane_halves(tokens):
    left = lax.broadcasted_iota(jnp.int32, (tokens, LANES), 1) < HEAD_DIM
    left = left.astype(jnp.float32)
    return left.astype(jnp.bfloat16), (1 - left).astype(jnp.bfloat16)


def tile_attention(packed, same_line, halves):
    tokens, width = packed.shape[0], packed.shape[1] // 3
    left, right = halves
    pieces = []
    for at in range(0, width, LANES):
        q = packed[:, at : at + LANES]
        k = packed[:, width + at : width + at + LANES]
        v = packed[:, 2 * width + at : 2 * width + at + LANES]
        scores = lax.dot_general(
            q,
            jnp.concatenate([k * left, k * right], axis=0),
            (((1,), (1,)), ((), ())),
            preferred_element_type=jnp.float32,
        )
        weights = []
        for head in range(2):
            own = jnp.where(same_line, scores[:, head * tokens : (head + 1) * tokens], HIDDEN)
            top = jnp.max(own, axis=-1, keepdims=True)
            weights.append(jnp.exp2(own - top).astype(jnp.bfloat16))
        values = jnp.concatenate(
            [
                jnp.concatenate([v * left, left], axis=1),
                jnp.concatenate([v * right, right], axis=1),
            ],
            axis=0,
        )
        mixed = jnp.dot(
            jnp.concatenate(weights, axis=1), values, preferred_element_type=jnp.float32
        )
        pieces.append((mixed[:, :LANES] / mixed[:, LANES:]).astype(jnp.bfloat16))
    return jnp.concatenate(pieces, axis=1)


def line_mask(tokens, line_of):
    rows = lax.broadcasted_iota(jnp.int32, (tokens, tokens), 0)
    columns = lax.broadcasted_iota(jnp.int32, (tokens, tokens), 1)
    return line_of(rows) == line_of(columns)


def project(normed, weight_ref, packed_ref, at):
    rows, width = normed.shape
    result = jnp.dot(normed, weight_ref[...], preferred_element_type=jnp.float32)
    scale = math.log2(math.e) / math.sqrt(HEAD_DIM)
    packed_ref[at : at + rows, :width] = (result[:, :width] * scale).astype(jnp.bfloat16)
    packed_ref[at : at + rows, width:] = result[:, width:].astype(jnp.bfloat16)


def lanes_of(value):
    return [value[:, at : at + LANES] for at in range(0, value.shape[1], LANES)]


def strided(ref, start, size, stride):
    return jnp.concatenate(
        [ref[at, pl.ds(start, size, stride=stride), :] for at in range(ref.shape[0])], axis=1
    )


def first_kernel(block, me_ref, x_hbm, gain_hbm, win_hbm, wout_hbm, *rest):
    n = len(rest) - 9
    outs = rest[:n]
    win, wout, natural, lined, packed, mixed, sems, x_ref, gain_ref = rest[n:]
    frames, columns, width = x_ref.shape
    tokens = frames * columns
    loads = [
        pltpu.make_async_copy(source, target, sems.at[index])
        for index, (source, target) in enumerate(
            (
                (x_hbm, x_ref),
                (gain_hbm, gain_ref),
                (win_hbm.at[block], win),
                (wout_hbm.at[block], wout),
            )
        )
    ]
    for load in loads:
        load.start()
    loads[0].wait()
    loads[1].wait()
    for at, lanes in enumerate(lanes_of(x_ref[...].reshape(tokens, width).astype(jnp.float32))):
        natural[at] = lanes
    gain = gain_ref[block : block + 1]
    group = 256 // frames
    for column in range(0, columns, group):
        pieces = []
        for each in range(column, column + group):
            floats = strided(natural, each, frames, columns)
            for at, lanes in enumerate(lanes_of(floats)):
                lined[at, each * frames : (each + 1) * frames] = lanes
            pieces.append(normalise(floats, gain))
        if column == 0:
            loads[2].wait()
        project(jnp.concatenate(pieces, axis=0), win, packed, column * frames)
    mask = line_mask(LANES, lambda i: i // frames)
    halves = lane_halves(LANES)
    for at in range(0, tokens, LANES):
        mixed[at : at + LANES] = tile_attention(packed[at : at + LANES], mask, halves)
    loads[3].wait()
    for at in range(0, tokens, 256):
        update = jnp.dot(mixed[at : at + 256], wout[...], preferred_element_type=jnp.float32)
        for index, lanes in enumerate(lanes_of(update)):
            lined[index, at : at + 256] += lanes
    piece = frames // n
    for k in range(n):
        start = jnp.bitwise_xor(me_ref[0], k) * piece
        for frame in range(piece):
            outs[k][frame] = strided(lined, start + frame, columns, frames).astype(jnp.bfloat16)


def load_all(pairs, sems):
    loads = [
        pltpu.make_async_copy(source, target, sems.at[index])
        for index, (source, target) in enumerate(pairs)
    ]
    for load in loads:
        load.start()
    return loads


def prepare(refs, gain, win, packed_ref, at):
    pieces, start, count = [], at, 0
    for index, ref in enumerate(refs):
        floats = ref[...].reshape(-1, ref.shape[-1]).astype(jnp.float32)
        pieces.append(normalise(floats, gain))
        count += floats.shape[0]
        if count >= 256 or index == len(refs) - 1:
            normed = jnp.concatenate(pieces, axis=0) if len(pieces) > 1 else pieces[0]
            project(normed, win, packed_ref, start)
            pieces, start, count = [], start + count, 0


def early_kernel(block, count, *rest):
    ins, (gain_hbm, win_hbm, wout_hbm) = rest[:count], rest[count : count + 3]
    packed, win, wout, gain_ref, sems = rest[count + 3 :]
    loads = load_all(
        ((gain_hbm, gain_ref), (win_hbm.at[block], win), (wout_hbm.at[block], wout)), sems
    )
    loads[0].wait()
    loads[1].wait()
    prepare(ins, gain_ref[block : block + 1], win, packed, 0)
    loads[2].wait()


def late_kernel(block, count, *rest):
    ins, (gain_ref, win, packed) = rest[:count], rest[count:]
    prepare(ins, gain_ref[block : block + 1], win, packed, 0)


def middle_kernel(block, counts, core_ref, *rest):
    n = sum(counts)
    ins = rest[:n]
    groups = rest[n : n + len(counts) - 1]
    gain_ref, win, wout, keep_ref, give_ref, packed, lined, mixed = rest[n + len(counts) - 1 :]
    frames, columns, width = ins[0].shape
    per = columns * frames
    last = n - counts[-1]
    prepare(ins[last:], gain_ref[block : block + 1], win, packed, 0)
    homes = []
    for group, count in zip((*groups, packed), counts):
        homes += [(group, index * per) for index in range(count)]
    share = LANES // n
    mask = line_mask(LANES, lambda i: i % share)
    halves = lane_halves(LANES)
    for at in range(0, per, share):
        tile = jnp.concatenate(
            [group[start + at : start + at + share] for group, start in homes], axis=0
        )
        result = tile_attention(tile, mask, halves)
        for k in range(n):
            mixed[k * per + at : k * per + at + share] = result[k * share : (k + 1) * share]
    for k in range(0, n, 2):
        update = jnp.dot(
            mixed[k * per : (k + 2) * per], wout[...], preferred_element_type=jnp.float32
        )
        for each in range(2):
            lined[(k + each) * per : (k + each + 1) * per] = (
                ins[k + each][...].reshape(per, width).astype(jnp.float32)
                + update[each * per : (each + 1) * per]
            ).astype(jnp.bfloat16)
    core = core_ref[0]
    for half in range(n // 2):
        mine = pl.ds(pl.multiple_of((2 * half + core) * per, per), per)
        other = pl.ds(pl.multiple_of((2 * half + 1 - core) * per, per), per)
        keep_ref[half] = lined[mine].reshape(frames, columns, width)
        give_ref[half] = lined[other].reshape(frames, columns, width)


def last_kernel(block, rows, keep_ref, got_ref, kept_packed, gain_ref, win, wout, *rest):
    outs = rest[: 2 * len(rows)]
    packed, mixed = rest[2 * len(rows) :]
    _, frames, columns, width = keep_ref.shape
    per = frames * columns
    tile = 2 * per
    gain = gain_ref[block : block + 1]
    prepare([got_ref.at[row] for row in rows], gain, win, packed, 0)
    mask = line_mask(LANES, lambda i: i // (2 * columns))
    halves = lane_halves(LANES)
    for index, row in enumerate(rows):
        for at in range(0, per, LANES // 2):
            strips = []
            for each in range(at, at + LANES // 2, columns):
                strips.append(kept_packed[row * per + each : row * per + each + columns])
                strips.append(packed[index * per + each : index * per + each + columns])
            start = index * tile + 2 * at
            mixed[start : start + LANES] = tile_attention(
                jnp.concatenate(strips, axis=0), mask, halves
            )
    for index, row in enumerate(rows):
        update = jnp.dot(
            mixed[index * tile : (index + 1) * tile],
            wout[...],
            preferred_element_type=jnp.float32,
        ).reshape(frames, 2 * columns, width)
        for half, ref in enumerate((keep_ref, got_ref)):
            outs[2 * index + half][...] = (
                ref[row].astype(jnp.float32) + update[:, half * columns : (half + 1) * columns]
            ).astype(jnp.bfloat16)


def join_kernel(starts_ref, *rest):
    pieces, out, sems = rest[:-2], rest[-2], rest[-1]
    size = pieces[0].shape[0]
    copies = []
    for index, piece in enumerate(pieces):
        where = pl.ds(starts_ref[index] * size, size)
        copies.append(pltpu.make_async_copy(piece, out.at[where], sems.at[index]))
        copies[-1].start()
    for copy in copies:
        copy.wait()


SMEM = pl.BlockSpec(memory_space=pltpu.SMEM)
VMEM = pl.BlockSpec(memory_space=pltpu.VMEM)
HBM = pl.BlockSpec(memory_space=pltpu.HBM)


def call(kernel, name, outs, in_specs, scratch_shapes, limit=24):
    return pl.pallas_call(
        kernel,
        out_shape=outs,
        in_specs=in_specs,
        out_specs=[VMEM] * len(outs),
        scratch_shapes=scratch_shapes,
        compiler_params=pltpu.CompilerParams(vmem_limit_bytes=limit << 20),
        name=name,
    )


def fast_body(n, video, norm_gain, qkv_weight, out_weight):
    frames, _, columns, width = video.shape
    piece = frames // n
    per = piece * columns
    tokens = frames * columns
    spot = lax.axis_index("aa")
    core = lax.axis_index("ba")
    bf16, f32 = jnp.bfloat16, jnp.float32
    array = jax.ShapeDtypeStruct
    message = array((piece, columns, width), bf16)
    win_shape, wout_shape = (width, 3 * width), (width, width)
    gain_shape = norm_gain.shape
    local = pltpu.with_memory_space_constraint(
        video.reshape(frames, columns, width), pltpu.HBM
    )
    weights = tuple(
        pltpu.with_memory_space_constraint(w, pltpu.HBM)
        for w in (norm_gain, qkv_weight, out_weight)
    )

    sent = call(
        functools.partial(first_kernel, 0),
        "first",
        [message] * n,
        [SMEM, HBM, HBM, HBM, HBM],
        [
            pltpu.VMEM(win_shape, bf16),
            pltpu.VMEM(wout_shape, bf16),
            pltpu.VMEM((width // LANES, tokens, LANES), f32),
            pltpu.VMEM((width // LANES, tokens, LANES), f32),
            pltpu.VMEM((tokens, 3 * width), bf16),
            pltpu.VMEM((tokens, width), bf16),
            pltpu.SemaphoreType.DMA((4,)),
            pltpu.VMEM((frames, columns, width), bf16),
            pltpu.VMEM(gain_shape, f32),
        ],
    )(spot[None], local, *weights)

    came = {0: sent[0]}
    for k in FIRST_ORDER if len(FIRST_ORDER) == n - 1 else range(1, n):
        came[k] = lax.ppermute(sent[k], "aa", [(i, i ^ k) for i in range(n)])

    def early(block, name, ins):
        return call(
            functools.partial(early_kernel, block, len(ins)),
            name,
            [
                array((sum(i.size for i in ins) // width, 3 * width), bf16),
                array(win_shape, bf16),
                array(wout_shape, bf16),
                array(gain_shape, f32),
            ],
            [VMEM] * len(ins) + [HBM, HBM, HBM],
            [pltpu.SemaphoreType.DMA((3,))],
        )(*ins, *weights)

    half, quarter = n // 2, n // 4
    packed_early, win, wout, gain = early(1, "early", [came[k] for k in range(half)])
    (packed_late,) = call(
        functools.partial(late_kernel, 1, quarter),
        "late",
        [array((quarter * per, 3 * width), bf16)],
        [VMEM] * (quarter + 2),
        [],
    )(*[came[k] for k in range(half, half + quarter)], gain, win)

    kept = array((n // 2, piece, columns, width), bf16)
    keep, give = call(
        functools.partial(middle_kernel, 1, (half, quarter, n - half - quarter)),
        "middle",
        [kept, kept],
        [SMEM] + [VMEM] * (n + 5),
        [
            pltpu.VMEM(((n - half - quarter) * per, 3 * width), bf16),
            pltpu.VMEM((tokens, width), bf16),
            pltpu.VMEM((tokens, width), bf16),
        ],
    )(core[None], *[came[k] for k in range(n)], packed_early, packed_late, gain, win, wout)

    got = lax.ppermute(give, "ba", [(0, 1), (1, 0)])
    kept_packed, win, wout, gain = early(2, "kept", [keep])

    arrived, starts = [], []
    for rows in LAST_ROWS if sum(map(len, LAST_ROWS)) == n // 2 else [[r] for r in range(n // 2)]:
        results = call(
            functools.partial(last_kernel, 2, rows),
            "last",
            [message] * (2 * len(rows)),
            [VMEM] * 6,
            [
                pltpu.VMEM((len(rows) * per, 3 * width), bf16),
                pltpu.VMEM((len(rows) * 2 * per, width), bf16),
            ],
        )(keep, got, kept_packed, gain, win, wout)
        for index, row in enumerate(rows):
            for swap in range(2):
                pairs = [
                    (2 * a + b, 2 * (a ^ (2 * row + b)) + (b ^ swap))
                    for a in range(n)
                    for b in range(2)
                ]
                arrived.append(lax.ppermute(results[2 * index + swap], ("aa", "ba"), pairs))
                starts.append(jnp.bitwise_xor(spot, 2 * row + jnp.bitwise_xor(core, swap)))

    out = pl.pallas_call(
        join_kernel,
        out_shape=jax.ShapeDtypeStruct((frames, columns, width), bf16),
        in_specs=[SMEM] + [VMEM] * n,
        out_specs=HBM,
        scratch_shapes=[pltpu.SemaphoreType.DMA((n,))],
        name="join",
        compiler_params=pltpu.CompilerParams(vmem_limit_bytes=4 << 20),
    )(jnp.stack(starts).astype(jnp.int32), *arrived)
    return out.reshape(video.shape)


def body(n, cores, video, norm_gain, qkv_weight, out_weight):
    frames, rows, columns, width = video.shape
    piece = frames // n
    fast = (
        cores == 2
        and rows == 1
        and n % 4 == 0
        and n & (n - 1) == 0
        and LANES % n == 0
        and (LANES // n) % 16 == 0
        and frames % n == 0
        and LANES % frames == 0
        and frames % 8 == 0
        and columns % 16 == 0
        and LANES % (2 * columns) == 0
        and (columns * piece) % LANES == 0
        and (frames * columns) % 256 == 0
        and width == HEADS * HEAD_DIM
        and width % LANES == 0
    )
    if fast:
        return fast_body(n, video, norm_gain, qkv_weight, out_weight)
    return general_body(video, norm_gain, qkv_weight, out_weight)


def solution(mesh):
    return jax.shard_map(
        functools.partial(body, mesh.shape["aa"], mesh.shape["ba"]),
        mesh=mesh,
        in_specs=(P("groups", "aa", "ba", None), P(), P(), P()),
        out_specs=P("groups", "aa", "ba", None),
        check_vma=False,
    )
```

```python
import functools
import math

import jax
import jax.numpy as jnp
from jax import lax
from jax.experimental import pallas as pl
from jax.experimental.pallas import tpu as pltpu
from jax.sharding import PartitionSpec as P


HEADS = 8
HEAD_DIM = 64
EPS = 1e-06
LANES = 128
HIDDEN = -1e30


score_forms = ("sbcnd,tbcnd->bcnst", "ascnd,atcnd->acnst", "absnd,abtnd->abnst")
mix_forms = ("bcnst,tbcnd->sbcnd", "acnst,atcnd->ascnd", "abnst,abtnd->absnd")


def attend(queries, key_rows, value_rows, line):
    shape = queries.shape
    split = shape[:3] + (HEADS, HEAD_DIM)
    scores = jnp.einsum(
        score_forms[line],
        queries.reshape(split),
        key_rows.reshape(split),
        preferred_element_type=jnp.float32,
    ) * (1.0 / math.sqrt(HEAD_DIM))
    weights = jax.nn.softmax(scores, axis=-1).astype(jnp.bfloat16)
    mixed = jnp.einsum(
        mix_forms[line], weights, value_rows.reshape(split), preferred_element_type=jnp.float32
    )
    return mixed.astype(jnp.bfloat16).reshape(shape)


def full_block(state, gain, weight_in, weight_out, line):
    floats = state.astype(jnp.float32)
    meansq = jnp.mean(floats * floats, axis=-1, keepdims=True)
    normed = (floats * lax.rsqrt(meansq + EPS) * gain).astype(jnp.bfloat16)
    packed = jnp.dot(normed, weight_in, preferred_element_type=jnp.float32).astype(jnp.bfloat16)
    width = state.shape[-1]
    mixed = attend(
        packed[..., :width], packed[..., width : 2 * width], packed[..., 2 * width :], line
    )
    update = jnp.dot(mixed, weight_out, preferred_element_type=jnp.float32)
    return (floats + update).astype(jnp.bfloat16)


def general_body(video, norm_gain, qkv_weight, out_weight):
    state = full_block(video, norm_gain[0], qkv_weight[0], out_weight[0], 0)
    state = lax.all_to_all(state, "aa", split_axis=0, concat_axis=1, tiled=True)
    state = full_block(state, norm_gain[1], qkv_weight[1], out_weight[1], 1)
    state = lax.all_to_all(state, "ba", split_axis=1, concat_axis=2, tiled=True)
    state = full_block(state, norm_gain[2], qkv_weight[2], out_weight[2], 2)
    state = lax.all_to_all(state, "ba", split_axis=2, concat_axis=1, tiled=True)
    return lax.all_to_all(state, "aa", split_axis=1, concat_axis=0, tiled=True)


def normalise(floats, gain):
    meansq = jnp.mean(floats * floats, axis=-1, keepdims=True)
    return (floats * lax.rsqrt(meansq + EPS) * gain).astype(jnp.bfloat16)


def lane_halves(tokens):
    left = lax.broadcasted_iota(jnp.int32, (tokens, LANES), 1) < HEAD_DIM
    left = left.astype(jnp.float32)
    return left.astype(jnp.bfloat16), (1 - left).astype(jnp.bfloat16)


def tile_attention(packed, same_line, halves):
    tokens, width = packed.shape[0], packed.shape[1] // 3
    left, right = halves
    pieces = []
    for at in range(0, width, LANES):
        q = packed[:, at : at + LANES]
        k = packed[:, width + at : width + at + LANES]
        v = packed[:, 2 * width + at : 2 * width + at + LANES]
        scores = lax.dot_general(
            q,
            jnp.concatenate([k * left, k * right], axis=0),
            (((1,), (1,)), ((), ())),
            preferred_element_type=jnp.float32,
        )
        weights = []
        for head in range(2):
            own = jnp.where(same_line, scores[:, head * tokens : (head + 1) * tokens], HIDDEN)
            top = jnp.max(own, axis=-1, keepdims=True)
            weights.append(jnp.exp2(own - top).astype(jnp.bfloat16))
        values = jnp.concatenate(
            [
                jnp.concatenate([v * left, left], axis=1),
                jnp.concatenate([v * right, right], axis=1),
            ],
            axis=0,
        )
        mixed = jnp.dot(
            jnp.concatenate(weights, axis=1), values, preferred_element_type=jnp.float32
        )
        pieces.append((mixed[:, :LANES] / mixed[:, LANES:]).astype(jnp.bfloat16))
    return jnp.concatenate(pieces, axis=1)


def line_mask(tokens, line_of):
    rows = lax.broadcasted_iota(jnp.int32, (tokens, tokens), 0)
    columns = lax.broadcasted_iota(jnp.int32, (tokens, tokens), 1)
    return line_of(rows) == line_of(columns)


def project(normed, weight_ref, packed_ref, at):
    rows, width = normed.shape
    result = jnp.dot(normed, weight_ref[...], preferred_element_type=jnp.float32)
    scale = math.log2(math.e) / math.sqrt(HEAD_DIM)
    packed_ref[at : at + rows, :width] = (result[:, :width] * scale).astype(jnp.bfloat16)
    packed_ref[at : at + rows, width:] = result[:, width:].astype(jnp.bfloat16)


def lanes_of(value):
    return [value[:, at : at + LANES] for at in range(0, value.shape[1], LANES)]


def strided(ref, start, size, stride):
    return jnp.concatenate(
        [ref[at, pl.ds(start, size, stride=stride), :] for at in range(ref.shape[0])], axis=1
    )


def first_kernel(block, me_ref, x_hbm, gain_hbm, win_hbm, wout_hbm, *rest):
    n = len(rest) - 9
    outs = rest[:n]
    win, wout, natural, lined, packed, mixed, sems, x_ref, gain_ref = rest[n:]
    frames, columns, width = x_ref.shape
    tokens = frames * columns
    loads = [
        pltpu.make_async_copy(source, target, sems.at[index])
        for index, (source, target) in enumerate(
            (
                (x_hbm, x_ref),
                (gain_hbm, gain_ref),
                (win_hbm.at[block], win),
                (wout_hbm.at[block], wout),
            )
        )
    ]
    for load in loads:
        load.start()
    loads[0].wait()
    loads[1].wait()
    for at, lanes in enumerate(lanes_of(x_ref[...].reshape(tokens, width).astype(jnp.float32))):
        natural[at] = lanes
    gain = gain_ref[block : block + 1]
    group = 256 // frames
    for column in range(0, columns, group):
        pieces = []
        for each in range(column, column + group):
            floats = strided(natural, each, frames, columns)
            for at, lanes in enumerate(lanes_of(floats)):
                lined[at, each * frames : (each + 1) * frames] = lanes
            pieces.append(normalise(floats, gain))
        if column == 0:
            loads[2].wait()
        project(jnp.concatenate(pieces, axis=0), win, packed, column * frames)
    mask = line_mask(LANES, lambda i: i // frames)
    halves = lane_halves(LANES)
    for at in range(0, tokens, LANES):
        mixed[at : at + LANES] = tile_attention(packed[at : at + LANES], mask, halves)
    loads[3].wait()
    for at in range(0, tokens, 256):
        update = jnp.dot(mixed[at : at + 256], wout[...], preferred_element_type=jnp.float32)
        for index, lanes in enumerate(lanes_of(update)):
            lined[index, at : at + 256] += lanes
    piece = frames // n
    for k in range(n):
        start = jnp.bitwise_xor(me_ref[0], k) * piece
        for frame in range(piece):
            outs[k][frame] = strided(lined, start + frame, columns, frames).astype(jnp.bfloat16)


def load_all(pairs, sems):
    loads = [
        pltpu.make_async_copy(source, target, sems.at[index])
        for index, (source, target) in enumerate(pairs)
    ]
    for load in loads:
        load.start()
    return loads


def prepare(refs, gain, win, packed_ref, at):
    pieces, start, count = [], at, 0
    for index, ref in enumerate(refs):
        floats = ref[...].reshape(-1, ref.shape[-1]).astype(jnp.float32)
        pieces.append(normalise(floats, gain))
        count += floats.shape[0]
        if count >= 256 or index == len(refs) - 1:
            normed = jnp.concatenate(pieces, axis=0) if len(pieces) > 1 else pieces[0]
            project(normed, win, packed_ref, start)
            pieces, start, count = [], start + count, 0


def early_kernel(block, count, *rest):
    ins, (gain_hbm, win_hbm, wout_hbm) = rest[:count], rest[count : count + 3]
    packed, win, wout, gain_ref, sems = rest[count + 3 :]
    loads = load_all(
        ((gain_hbm, gain_ref), (win_hbm.at[block], win), (wout_hbm.at[block], wout)), sems
    )
    loads[0].wait()
    loads[1].wait()
    prepare(ins, gain_ref[block : block + 1], win, packed, 0)
    loads[2].wait()


def late_kernel(block, count, *rest):
    ins, (gain_ref, win, win_hbm, wout_hbm, packed, next_win, next_wout, sems) = (
        rest[:count],
        rest[count:],
    )
    loads = load_all(
        ((win_hbm.at[block + 1], next_win), (wout_hbm.at[block + 1], next_wout)), sems
    )
    prepare(ins, gain_ref[block : block + 1], win, packed, 0)
    for load in loads:
        load.wait()


def share_rows(core_ref, update, ins, keep, give):
    frames, columns, width = ins[0].shape
    per = frames * columns
    totals = [
        (ins[each][...].reshape(per, width).astype(jnp.float32) + update[each * per : (each + 1) * per])
        .astype(jnp.bfloat16)
        .reshape(frames, columns, width)
        for each in range(2)
    ]
    second = core_ref[0]

    @pl.when(second == 0)
    def _():
        keep[...] = totals[0]
        give[...] = totals[1]

    @pl.when(second != 0)
    def _():
        keep[...] = totals[1]
        give[...] = totals[0]


def middle_kernel(block, counts, pair, core_ref, *rest):
    n = sum(counts)
    ins = rest[:n]
    groups = rest[n : n + len(counts) - 1]
    gain_ref, win, wout, mixed, keep_ref, give_ref, packed = rest[n + len(counts) - 1 :]
    frames, columns, _ = ins[0].shape
    per = columns * frames
    last = n - counts[-1]
    prepare(ins[last:], gain_ref[block : block + 1], win, packed, 0)
    homes = []
    for group, count in zip((*groups, packed), counts):
        homes += [(group, index * per) for index in range(count)]
    share = LANES // n
    mask = line_mask(LANES, lambda i: i % share)
    halves = lane_halves(LANES)
    for at in range(0, per, share):
        tile = jnp.concatenate(
            [group[start + at : start + at + share] for group, start in homes], axis=0
        )
        result = tile_attention(tile, mask, halves)
        for k in range(n):
            mixed[k * per + at : k * per + at + share] = result[k * share : (k + 1) * share]
    k = 2 * pair
    update = jnp.dot(mixed[k * per : (k + 2) * per], wout[...], preferred_element_type=jnp.float32)
    share_rows(core_ref, update, ins[k : k + 2], keep_ref.at[0], give_ref.at[0])


def middle_rest_kernel(pairs, core_ref, mixed, wout, *rest):
    ins = rest[: 2 * len(pairs)]
    keep_ref, give_ref = rest[2 * len(pairs) :]
    frames, columns, _ = ins[0].shape
    per = columns * frames
    for index, pair in enumerate(pairs):
        k = 2 * pair
        update = jnp.dot(
            mixed[k * per : (k + 2) * per], wout[...], preferred_element_type=jnp.float32
        )
        share_rows(
            core_ref,
            update,
            ins[2 * index : 2 * index + 2],
            keep_ref.at[index],
            give_ref.at[index],
        )


def kept_kernel(block, keep_ref, gain_ref, win, packed):
    prepare(
        [keep_ref.at[row] for row in range(keep_ref.shape[0])],
        gain_ref[block : block + 1],
        win,
        packed,
        0,
    )


def last_kernel(block, rows, keep_ref, got_ref, kept_packed, gain_ref, win, wout, *rest):
    outs = rest[: 2 * len(rows)]
    packed, mixed = rest[2 * len(rows) :]
    _, frames, columns, width = keep_ref.shape
    per = frames * columns
    tile = 2 * per
    gain = gain_ref[block : block + 1]
    prepare([got_ref.at[row] for row in rows], gain, win, packed, 0)
    mask = line_mask(LANES, lambda i: i // (2 * columns))
    halves = lane_halves(LANES)
    for index, row in enumerate(rows):
        for at in range(0, per, LANES // 2):
            strips = []
            for each in range(at, at + LANES // 2, columns):
                strips.append(kept_packed[row * per + each : row * per + each + columns])
                strips.append(packed[index * per + each : index * per + each + columns])
            start = index * tile + 2 * at
            mixed[start : start + LANES] = tile_attention(
                jnp.concatenate(strips, axis=0), mask, halves
            )
    for index, row in enumerate(rows):
        update = jnp.dot(
            mixed[index * tile : (index + 1) * tile],
            wout[...],
            preferred_element_type=jnp.float32,
        ).reshape(frames, 2 * columns, width)
        for half, ref in enumerate((keep_ref, got_ref)):
            outs[2 * index + half][...] = (
                ref[row].astype(jnp.float32) + update[:, half * columns : (half + 1) * columns]
            ).astype(jnp.bfloat16)


def join_kernel(count, starts_ref, *rest):
    pieces, out, sems = rest[:count], rest[-2], rest[-1]
    size = pieces[0].shape[0]
    copies = []
    for index, piece in enumerate(pieces):
        where = pl.ds(starts_ref[index] * size, size)
        copies.append(pltpu.make_async_copy(piece, out.at[where], sems.at[index]))
        copies[-1].start()
    for copy in copies:
        copy.wait()


SMEM = pl.BlockSpec(memory_space=pltpu.SMEM)
VMEM = pl.BlockSpec(memory_space=pltpu.VMEM)
HBM = pl.BlockSpec(memory_space=pltpu.HBM)


def call(kernel, outs, in_specs, scratch_shapes, limit=24):
    return pl.pallas_call(
        kernel,
        out_shape=outs,
        in_specs=in_specs,
        out_specs=[VMEM] * len(outs),
        scratch_shapes=scratch_shapes,
        compiler_params=pltpu.CompilerParams(vmem_limit_bytes=limit << 20),
    )


def fast_body(n, video, norm_gain, qkv_weight, out_weight):
    frames, _, columns, width = video.shape
    piece = frames // n
    per = piece * columns
    tokens = frames * columns
    spot = lax.axis_index("aa")
    core = lax.axis_index("ba")
    bf16, f32 = jnp.bfloat16, jnp.float32
    array = jax.ShapeDtypeStruct
    message = array((piece, columns, width), bf16)
    win_shape, wout_shape = (width, 3 * width), (width, width)
    gain_shape = norm_gain.shape
    local = pltpu.with_memory_space_constraint(
        video.reshape(frames, columns, width), pltpu.HBM
    )
    weights = tuple(
        pltpu.with_memory_space_constraint(w, pltpu.HBM)
        for w in (norm_gain, qkv_weight, out_weight)
    )

    sent = call(
        functools.partial(first_kernel, 0),
        [message] * n,
        [SMEM, HBM, HBM, HBM, HBM],
        [
            pltpu.VMEM(win_shape, bf16),
            pltpu.VMEM(wout_shape, bf16),
            pltpu.VMEM((width // LANES, tokens, LANES), f32),
            pltpu.VMEM((width // LANES, tokens, LANES), f32),
            pltpu.VMEM((tokens, 3 * width), bf16),
            pltpu.VMEM((tokens, width), bf16),
            pltpu.SemaphoreType.DMA((4,)),
            pltpu.VMEM((frames, columns, width), bf16),
            pltpu.VMEM(gain_shape, f32),
        ],
    )(spot[None], local, *weights)

    came = {0: sent[0]}
    for k in range(1, n):
        came[k] = lax.ppermute(sent[k], "aa", [(i, i ^ k) for i in range(n)])

    half, quarter = n // 2, n // 4
    final = n - half - quarter
    packed_early, win, wout, gain = call(
        functools.partial(early_kernel, 1, half),
        [
            array((half * per, 3 * width), bf16),
            array(win_shape, bf16),
            array(wout_shape, bf16),
            array(gain_shape, f32),
        ],
        [VMEM] * half + [HBM, HBM, HBM],
        [pltpu.SemaphoreType.DMA((3,))],
    )(*[came[k] for k in range(half)], *weights)
    packed_late, next_win, next_wout = call(
        functools.partial(late_kernel, 1, quarter),
        [array((quarter * per, 3 * width), bf16), array(win_shape, bf16), array(wout_shape, bf16)],
        [VMEM] * (quarter + 2) + [HBM, HBM],
        [pltpu.SemaphoreType.DMA((2,))],
    )(*[came[k] for k in range(half, half + quarter)], gain, win, *weights[1:])

    lead, *others = row_order(n)

    def kept(count):
        return array((count, piece, columns, width), bf16)

    mixed, keep, give = call(
        functools.partial(middle_kernel, 1, (half, quarter, final), lead),
        [array((tokens, width), bf16), kept(1), kept(1)],
        [SMEM] + [VMEM] * (n + 5),
        [pltpu.VMEM((final * per, 3 * width), bf16)],
    )(core[None], *[came[k] for k in range(n)], packed_early, packed_late, gain, win, wout)

    arrived, starts = [], []

    def swap(value):
        return lax.ppermute(value, "ba", [(0, 1), (1, 0)])

    def project_kept(value):
        count = value.shape[0]
        (packed,) = call(
            functools.partial(kept_kernel, 2),
            [array((count * per, 3 * width), bf16)],
            [VMEM] * 3,
            [],
        )(value, gain, next_win)
        return packed

    def finish(rows, pairs_of_rows, value, other, packed):
        results = call(
            functools.partial(last_kernel, 2, rows),
            [message] * (2 * len(rows)),
            [VMEM] * 6,
            [
                pltpu.VMEM((len(rows) * per, 3 * width), bf16),
                pltpu.VMEM((len(rows) * 2 * per, width), bf16),
            ],
        )(value, other, packed, gain, next_win, next_wout)
        for index, row in enumerate(pairs_of_rows):
            for flip in range(2):
                route = [
                    (2 * a + b, 2 * (a ^ (2 * row + b)) + (b ^ flip))
                    for a in range(n)
                    for b in range(2)
                ]
                arrived.append(lax.ppermute(results[2 * index + flip], ("aa", "ba"), route))
                starts.append(jnp.bitwise_xor(spot, 2 * row + jnp.bitwise_xor(core, flip)))

    got = swap(give)
    finish([0], [lead], keep, got, project_kept(keep))

    keep, give = call(
        functools.partial(middle_rest_kernel, others),
        [kept(len(others)), kept(len(others))],
        [SMEM] + [VMEM] * (2 + 2 * len(others)),
        [],
    )(
        core[None],
        mixed,
        wout,
        *[came[2 * pair + each] for pair in others for each in range(2)],
    )
    got = swap(give)
    packed = project_kept(keep)
    cut = n // 4 - 1
    for rows in ([*range(cut)], [*range(cut, len(others))]):
        finish(rows, [others[row] for row in rows], keep, got, packed)

    def join(values, offsets, base=None):
        count = len(values)
        given = [] if base is None else [base]
        return pl.pallas_call(
            functools.partial(join_kernel, count),
            out_shape=array((frames, columns, width), bf16),
            in_specs=[SMEM] + [VMEM] * count + [HBM] * len(given),
            out_specs=HBM,
            scratch_shapes=[pltpu.SemaphoreType.DMA((count,))],
            input_output_aliases={count + 1: 0} if given else {},
            name="join",
            compiler_params=pltpu.CompilerParams(vmem_limit_bytes=4 << 20),
        )(jnp.stack(offsets).astype(jnp.int32), *values, *given)

    out = join(arrived[:2], starts[:2])
    out = join(arrived[2:], starts[2:], out)
    return out.reshape(video.shape)


def body(n, cores, video, norm_gain, qkv_weight, out_weight):
    frames, rows, columns, width = video.shape
    piece = frames // n
    fast = (
        cores == 2
        and rows == 1
        and n % 4 == 0
        and n & (n - 1) == 0
        and LANES % n == 0
        and (LANES // n) % 16 == 0
        and frames % n == 0
        and LANES % frames == 0
        and frames % 8 == 0
        and columns % 16 == 0
        and LANES % (2 * columns) == 0
        and (columns * piece) % LANES == 0
        and (frames * columns) % 256 == 0
        and width == HEADS * HEAD_DIM
        and width % LANES == 0
    )
    if fast:
        return fast_body(n, video, norm_gain, qkv_weight, out_weight)
    return general_body(video, norm_gain, qkv_weight, out_weight)


def row_order(n):
    return [*range(n // 4, n // 2), *range(n // 4 - 1, -1, -1)]


def solution(mesh):
    n = mesh.shape["aa"]
    return jax.shard_map(
        functools.partial(body, n, mesh.shape["ba"]),
        mesh=mesh,
        in_specs=(P("groups", "aa", "ba", None), P(), P(), P()),
        out_specs=P("groups", "aa", "ba", None),
        check_vma=False,
    )
```

```python
import functools
import math

import jax
import jax.numpy as jnp
from jax import lax
from jax.experimental import pallas as pl
from jax.experimental.pallas import tpu as pltpu
from jax.sharding import PartitionSpec as P


HEADS = 8
HEAD_DIM = 64
EPS = 1e-06
LANES = 128
HIDDEN = -1e30


score_forms = ("sbcnd,tbcnd->bcnst", "ascnd,atcnd->acnst", "absnd,abtnd->abnst")
mix_forms = ("bcnst,tbcnd->sbcnd", "acnst,atcnd->ascnd", "abnst,abtnd->absnd")


def attend(queries, key_rows, value_rows, line):
    shape = queries.shape
    split = shape[:3] + (HEADS, HEAD_DIM)
    scores = jnp.einsum(
        score_forms[line],
        queries.reshape(split),
        key_rows.reshape(split),
        preferred_element_type=jnp.float32,
    ) * (1.0 / math.sqrt(HEAD_DIM))
    weights = jax.nn.softmax(scores, axis=-1).astype(jnp.bfloat16)
    mixed = jnp.einsum(
        mix_forms[line], weights, value_rows.reshape(split), preferred_element_type=jnp.float32
    )
    return mixed.astype(jnp.bfloat16).reshape(shape)


def full_block(state, gain, weight_in, weight_out, line):
    floats = state.astype(jnp.float32)
    meansq = jnp.mean(floats * floats, axis=-1, keepdims=True)
    normed = (floats * lax.rsqrt(meansq + EPS) * gain).astype(jnp.bfloat16)
    packed = jnp.dot(normed, weight_in, preferred_element_type=jnp.float32).astype(jnp.bfloat16)
    width = state.shape[-1]
    mixed = attend(
        packed[..., :width], packed[..., width : 2 * width], packed[..., 2 * width :], line
    )
    update = jnp.dot(mixed, weight_out, preferred_element_type=jnp.float32)
    return (floats + update).astype(jnp.bfloat16)


def general_body(video, norm_gain, qkv_weight, out_weight):
    state = full_block(video, norm_gain[0], qkv_weight[0], out_weight[0], 0)
    state = lax.all_to_all(state, "aa", split_axis=0, concat_axis=1, tiled=True)
    state = full_block(state, norm_gain[1], qkv_weight[1], out_weight[1], 1)
    state = lax.all_to_all(state, "ba", split_axis=1, concat_axis=2, tiled=True)
    state = full_block(state, norm_gain[2], qkv_weight[2], out_weight[2], 2)
    state = lax.all_to_all(state, "ba", split_axis=2, concat_axis=1, tiled=True)
    return lax.all_to_all(state, "aa", split_axis=1, concat_axis=0, tiled=True)


def normalise(floats, gain):
    meansq = jnp.mean(floats * floats, axis=-1, keepdims=True)
    return (floats * lax.rsqrt(meansq + EPS) * gain).astype(jnp.bfloat16)


def lane_halves(tokens):
    left = lax.broadcasted_iota(jnp.int32, (tokens, LANES), 1) < HEAD_DIM
    left = left.astype(jnp.float32)
    return left.astype(jnp.bfloat16), (1 - left).astype(jnp.bfloat16)


def tile_attention(packed, same_line, halves):
    tokens, width = packed.shape[0], packed.shape[1] // 3
    left, right = halves
    pieces = []
    for at in range(0, width, LANES):
        q = packed[:, at : at + LANES]
        k = packed[:, width + at : width + at + LANES]
        v = packed[:, 2 * width + at : 2 * width + at + LANES]
        scores = lax.dot_general(
            q,
            jnp.concatenate([k * left, k * right], axis=0),
            (((1,), (1,)), ((), ())),
            preferred_element_type=jnp.float32,
        )
        weights = []
        for head in range(2):
            own = jnp.where(same_line, scores[:, head * tokens : (head + 1) * tokens], HIDDEN)
            top = jnp.max(own, axis=-1, keepdims=True)
            weights.append(jnp.exp2(own - top).astype(jnp.bfloat16))
        values = jnp.concatenate(
            [
                jnp.concatenate([v * left, left], axis=1),
                jnp.concatenate([v * right, right], axis=1),
            ],
            axis=0,
        )
        mixed = jnp.dot(
            jnp.concatenate(weights, axis=1), values, preferred_element_type=jnp.float32
        )
        pieces.append((mixed[:, :LANES] / mixed[:, LANES:]).astype(jnp.bfloat16))
    return jnp.concatenate(pieces, axis=1)


def line_mask(tokens, line_of):
    rows = lax.broadcasted_iota(jnp.int32, (tokens, tokens), 0)
    columns = lax.broadcasted_iota(jnp.int32, (tokens, tokens), 1)
    return line_of(rows) == line_of(columns)


def project(normed, weight_ref, packed_ref, at):
    rows, width = normed.shape
    result = jnp.dot(normed, weight_ref[...], preferred_element_type=jnp.float32)
    scale = math.log2(math.e) / math.sqrt(HEAD_DIM)
    packed_ref[at : at + rows, :width] = (result[:, :width] * scale).astype(jnp.bfloat16)
    packed_ref[at : at + rows, width:] = result[:, width:].astype(jnp.bfloat16)


def lanes_of(value):
    return [value[:, at : at + LANES] for at in range(0, value.shape[1], LANES)]


def strided(ref, start, size, stride):
    return jnp.concatenate(
        [ref[at, pl.ds(start, size, stride=stride), :] for at in range(ref.shape[0])], axis=1
    )


def first_kernel(block, x_hbm, gain_hbm, win_hbm, wout_hbm, *rest):
    n = len(rest) - 9
    outs = rest[:n]
    win, wout, natural, lined, packed, mixed, sems, x_ref, gain_ref = rest[n:]
    frames, columns, width = x_ref.shape
    tokens = frames * columns
    loads = [
        pltpu.make_async_copy(source, target, sems.at[index])
        for index, (source, target) in enumerate(
            (
                (x_hbm, x_ref),
                (gain_hbm, gain_ref),
                (win_hbm.at[block], win),
                (wout_hbm.at[block], wout),
            )
        )
    ]
    for load in loads:
        load.start()
    loads[0].wait()
    loads[1].wait()
    for at, lanes in enumerate(lanes_of(x_ref[...].reshape(tokens, width).astype(jnp.float32))):
        natural[at] = lanes
    gain = gain_ref[block : block + 1]
    group = 256 // frames
    for column in range(0, columns, group):
        pieces = []
        for each in range(column, column + group):
            floats = strided(natural, each, frames, columns)
            for at, lanes in enumerate(lanes_of(floats)):
                lined[at, each * frames : (each + 1) * frames] = lanes
            pieces.append(normalise(floats, gain))
        if column == 0:
            loads[2].wait()
        project(jnp.concatenate(pieces, axis=0), win, packed, column * frames)
    mask = line_mask(LANES, lambda i: i // frames)
    halves = lane_halves(LANES)
    for at in range(0, tokens, LANES):
        mixed[at : at + LANES] = tile_attention(packed[at : at + LANES], mask, halves)
    loads[3].wait()
    for at in range(0, tokens, 256):
        update = jnp.dot(mixed[at : at + 256], wout[...], preferred_element_type=jnp.float32)
        for index, lanes in enumerate(lanes_of(update)):
            lined[index, at : at + 256] += lanes
    piece = frames // n
    spot = lax.axis_index("aa")
    for k in range(n):
        start = jnp.bitwise_xor(spot, k) * piece
        for frame in range(piece):
            outs[k][frame] = strided(lined, start + frame, columns, frames).astype(jnp.bfloat16)


def load_all(pairs, sems):
    loads = [
        pltpu.make_async_copy(source, target, sems.at[index])
        for index, (source, target) in enumerate(pairs)
    ]
    for load in loads:
        load.start()
    return loads


def prepare(refs, gain, win, packed_ref, at):
    pieces, start, count = [], at, 0
    for index, ref in enumerate(refs):
        floats = ref[...].reshape(-1, ref.shape[-1]).astype(jnp.float32)
        pieces.append(normalise(floats, gain))
        count += floats.shape[0]
        if count >= 256 or index == len(refs) - 1:
            normed = jnp.concatenate(pieces, axis=0) if len(pieces) > 1 else pieces[0]
            project(normed, win, packed_ref, start)
            pieces, start, count = [], start + count, 0


def weights_kernel(blocks, gain_hbm, win_hbm, wout_hbm, *rest):
    gain, copies, sems = rest[0], rest[1:-1], rest[-1]
    pairs = [(gain_hbm, gain)]
    for index, block in enumerate(blocks):
        pairs += [
            (win_hbm.at[block], copies[2 * index]),
            (wout_hbm.at[block], copies[2 * index + 1]),
        ]
    for load in load_all(pairs, sems):
        load.wait()


def group_kernel(block, count, *rest):
    ins, (gain_ref, win, packed) = rest[:count], rest[count:]
    prepare(ins, gain_ref[block : block + 1], win, packed, 0)


def share_rows(update, ins, keep, give):
    frames, columns, width = ins[0].shape
    per = frames * columns
    totals = [
        (ins[each][...].reshape(per, width).astype(jnp.float32) + update[each * per : (each + 1) * per])
        .astype(jnp.bfloat16)
        .reshape(frames, columns, width)
        for each in range(2)
    ]
    second = lax.axis_index("ba")

    @pl.when(second == 0)
    def _():
        keep[...] = totals[0]
        give[...] = totals[1]

    @pl.when(second != 0)
    def _():
        keep[...] = totals[1]
        give[...] = totals[0]


def middle_kernel(block, groups, pair, *rest):
    n = sum(map(len, groups))
    ins = rest[:n]
    ready = rest[n : n + len(groups) - 1]
    gain_ref, win, wout, mixed, keep_ref, give_ref, packed = rest[n + len(groups) - 1 :]
    frames, columns, _ = ins[0].shape
    per = columns * frames
    prepare([ins[k] for k in groups[-1]], gain_ref[block : block + 1], win, packed, 0)
    homes = [None] * n
    for group, ref in zip(groups, (*ready, packed)):
        for index, k in enumerate(group):
            homes[k] = (ref, index * per)
    share = LANES // n
    mask = line_mask(LANES, lambda i: i % share)
    halves = lane_halves(LANES)
    for at in range(0, per, share):
        tile = jnp.concatenate(
            [group[start + at : start + at + share] for group, start in homes], axis=0
        )
        result = tile_attention(tile, mask, halves)
        for k in range(n):
            mixed[k * per + at : k * per + at + share] = result[k * share : (k + 1) * share]
    k = 2 * pair
    update = jnp.dot(mixed[k * per : (k + 2) * per], wout[...], preferred_element_type=jnp.float32)
    share_rows(update, ins[k : k + 2], keep_ref.at[0], give_ref.at[0])


def middle_rest_kernel(pairs, mixed, wout, *rest):
    ins = rest[: 2 * len(pairs)]
    keep_ref, give_ref = rest[2 * len(pairs) :]
    frames, columns, _ = ins[0].shape
    per = columns * frames
    for index, pair in enumerate(pairs):
        k = 2 * pair
        update = jnp.dot(
            mixed[k * per : (k + 2) * per], wout[...], preferred_element_type=jnp.float32
        )
        share_rows(
            update,
            ins[2 * index : 2 * index + 2],
            keep_ref.at[index],
            give_ref.at[index],
        )


def kept_kernel(block, keep_ref, gain_ref, win, packed):
    prepare(
        [keep_ref.at[row] for row in range(keep_ref.shape[0])],
        gain_ref[block : block + 1],
        win,
        packed,
        0,
    )


def last_kernel(block, rows, keep_ref, got_ref, kept_packed, gain_ref, win, wout, *rest):
    outs = rest[: 2 * len(rows)]
    packed, mixed = rest[2 * len(rows) :]
    _, frames, columns, width = keep_ref.shape
    per = frames * columns
    tile = 2 * per
    gain = gain_ref[block : block + 1]
    prepare([got_ref.at[row] for row in rows], gain, win, packed, 0)
    mask = line_mask(LANES, lambda i: i // (2 * columns))
    halves = lane_halves(LANES)
    for index, row in enumerate(rows):
        for at in range(0, per, LANES // 2):
            strips = []
            for each in range(at, at + LANES // 2, columns):
                strips.append(kept_packed[row * per + each : row * per + each + columns])
                strips.append(packed[index * per + each : index * per + each + columns])
            start = index * tile + 2 * at
            mixed[start : start + LANES] = tile_attention(
                jnp.concatenate(strips, axis=0), mask, halves
            )
    for index, row in enumerate(rows):
        update = jnp.dot(
            mixed[index * tile : (index + 1) * tile],
            wout[...],
            preferred_element_type=jnp.float32,
        ).reshape(frames, 2 * columns, width)
        for half, ref in enumerate((keep_ref, got_ref)):
            outs[2 * index + half][...] = (
                ref[row].astype(jnp.float32) + update[:, half * columns : (half + 1) * columns]
            ).astype(jnp.bfloat16)


def join_kernel(senders, *rest):
    pieces, out, sems = rest[: len(senders)], rest[-2], rest[-1]
    size = pieces[0].shape[0]
    spot, core = lax.axis_index("aa"), lax.axis_index("ba")
    copies = []
    for index, (piece, (row, flip)) in enumerate(zip(pieces, senders)):
        sender = jnp.bitwise_xor(spot, 2 * row + jnp.bitwise_xor(core, flip))
        where = pl.ds(sender * size, size)
        copies.append(pltpu.make_async_copy(piece, out.at[where], sems.at[index]))
        copies[-1].start()
    for copy in copies:
        copy.wait()


VMEM = pl.BlockSpec(memory_space=pltpu.VMEM)
HBM = pl.BlockSpec(memory_space=pltpu.HBM)


def call(kernel, outs, in_specs, scratch_shapes, limit=8):
    return pl.pallas_call(
        kernel,
        out_shape=outs,
        in_specs=in_specs,
        out_specs=[VMEM] * len(outs),
        scratch_shapes=scratch_shapes,
        compiler_params=pltpu.CompilerParams(vmem_limit_bytes=limit << 20),
    )


def fast_body(n, video, norm_gain, qkv_weight, out_weight):
    frames, _, columns, width = video.shape
    piece = frames // n
    per = piece * columns
    tokens = frames * columns
    bf16, f32 = jnp.bfloat16, jnp.float32
    array = jax.ShapeDtypeStruct
    message = array((piece, columns, width), bf16)
    win_shape, wout_shape = (width, 3 * width), (width, width)
    gain_shape = norm_gain.shape
    local = pltpu.with_memory_space_constraint(
        video.reshape(frames, columns, width), pltpu.HBM
    )
    weights = tuple(
        pltpu.with_memory_space_constraint(w, pltpu.HBM)
        for w in (norm_gain, qkv_weight, out_weight)
    )

    sent = call(
        functools.partial(first_kernel, 0),
        [message] * n,
        [HBM] * 4,
        [
            pltpu.VMEM(win_shape, bf16),
            pltpu.VMEM(wout_shape, bf16),
            pltpu.VMEM((width // LANES, tokens, LANES), f32),
            pltpu.VMEM((width // LANES, tokens, LANES), f32),
            pltpu.VMEM((tokens, 3 * width), bf16),
            pltpu.VMEM((tokens, width), bf16),
            pltpu.SemaphoreType.DMA((4,)),
            pltpu.VMEM((frames, columns, width), bf16),
            pltpu.VMEM(gain_shape, f32),
        ],
        limit=24,
    )(local, *weights)

    came = {0: sent[0]}
    for k in range(1, n):
        came[k] = lax.ppermute(sent[k], "aa", [(i, i ^ k) for i in range(n)])

    later = range(1, norm_gain.shape[0])
    gain, *fetched = call(
        functools.partial(weights_kernel, later),
        [array(gain_shape, f32)] + [array(win_shape, bf16), array(wout_shape, bf16)] * len(later),
        [HBM] * 3,
        [pltpu.SemaphoreType.DMA((1 + 2 * len(later),))],
    )(*weights)
    win, wout, next_win, next_wout = fetched

    *groups, final = arrival_groups(n)
    ready = []
    for group in groups:
        ready += call(
            functools.partial(group_kernel, 1, len(group)),
            [array((len(group) * per, 3 * width), bf16)],
            [VMEM] * (len(group) + 2),
            [],
        )(*[came[k] for k in group], gain, win)

    lead, *others = row_order(n)

    def kept(count):
        return array((count, piece, columns, width), bf16)

    mixed, keep, give = call(
        functools.partial(middle_kernel, 1, (*groups, final), lead),
        [array((tokens, width), bf16), kept(1), kept(1)],
        [VMEM] * (n + len(ready) + 3),
        [pltpu.VMEM((len(final) * per, 3 * width), bf16)],
    )(*[came[k] for k in range(n)], *ready, gain, win, wout)

    arrived, starts = [], []

    def swap(value):
        return lax.ppermute(value, "ba", [(0, 1), (1, 0)])

    def project_kept(value):
        count = value.shape[0]
        (packed,) = call(
            functools.partial(kept_kernel, 2),
            [array((count * per, 3 * width), bf16)],
            [VMEM] * 3,
            [],
        )(value, gain, next_win)
        return packed

    def finish(rows, pairs_of_rows, value, other, packed):
        results = call(
            functools.partial(last_kernel, 2, rows),
            [message] * (2 * len(rows)),
            [VMEM] * 6,
            [
                pltpu.VMEM((len(rows) * per, 3 * width), bf16),
                pltpu.VMEM((len(rows) * 2 * per, width), bf16),
            ],
        )(value, other, packed, gain, next_win, next_wout)
        for index, row in enumerate(pairs_of_rows):
            for flip in range(2):
                route = [
                    (2 * a + b, 2 * (a ^ (2 * row + b)) + (b ^ flip))
                    for a in range(n)
                    for b in range(2)
                ]
                arrived.append(lax.ppermute(results[2 * index + flip], ("aa", "ba"), route))
                starts.append((row, flip))

    got = swap(give)
    finish([0], [lead], keep, got, project_kept(keep))

    keep, give = call(
        functools.partial(middle_rest_kernel, others),
        [kept(len(others)), kept(len(others))],
        [VMEM] * (2 + 2 * len(others)),
        [],
    )(
        mixed,
        wout,
        *[came[2 * pair + each] for pair in others for each in range(2)],
    )
    got = swap(give)
    packed = project_kept(keep)
    cut = n // 4 - 1
    for rows in ([*range(cut)], [*range(cut, len(others))]):
        finish(rows, [others[row] for row in rows], keep, got, packed)

    def join(values, senders, base=None):
        count = len(values)
        given = [] if base is None else [base]
        return pl.pallas_call(
            functools.partial(join_kernel, senders),
            out_shape=array((frames, columns, width), bf16),
            in_specs=[VMEM] * count + [HBM] * len(given),
            out_specs=HBM,
            scratch_shapes=[pltpu.SemaphoreType.DMA((count,))],
            input_output_aliases={count: 0} if given else {},
            name="join",
            compiler_params=pltpu.CompilerParams(vmem_limit_bytes=4 << 20),
        )(*values, *given)

    out = join(arrived[:2], starts[:2])
    out = join(arrived[2:], starts[2:], out)
    return out.reshape(video.shape)


def body(n, cores, video, norm_gain, qkv_weight, out_weight):
    frames, rows, columns, width = video.shape
    piece = frames // n
    fast = (
        cores == 2
        and rows == 1
        and n % 4 == 0
        and n & (n - 1) == 0
        and LANES % n == 0
        and (LANES // n) % 16 == 0
        and frames % n == 0
        and LANES % frames == 0
        and frames % 8 == 0
        and columns % 16 == 0
        and LANES % (2 * columns) == 0
        and (columns * piece) % LANES == 0
        and (frames * columns) % 256 == 0
        and width == HEADS * HEAD_DIM
        and width % LANES == 0
    )
    if fast:
        return fast_body(n, video, norm_gain, qkv_weight, out_weight)
    return general_body(video, norm_gain, qkv_weight, out_weight)


def row_order(n):
    return [*range(n // 4, n // 2), *range(n // 4 - 1, -1, -1)]


def arrival_groups(n):
    half, quarter = n // 2, n // 4
    return [
        [0, 1, *range(half, half + quarter)],
        [*range(2, half)],
        [*range(half + quarter, n)],
    ]


def solution(mesh):
    n = mesh.shape["aa"]
    return jax.shard_map(
        functools.partial(body, n, mesh.shape["ba"]),
        mesh=mesh,
        in_specs=(P("groups", "aa", "ba", None), P(), P(), P()),
        out_specs=P("groups", "aa", "ba", None),
        check_vma=False,
    )
```

```python
import functools
import math

import jax
import jax.numpy as jnp
from jax import lax
from jax.experimental import pallas as pl
from jax.experimental.pallas import tpu as pltpu
from jax.sharding import PartitionSpec as P


HEADS = 8
HEAD_DIM = 64
EPS = 1e-06
LANES = 128
HIDDEN = -1e30


score_forms = ("sbcnd,tbcnd->bcnst", "ascnd,atcnd->acnst", "absnd,abtnd->abnst")
mix_forms = ("bcnst,tbcnd->sbcnd", "acnst,atcnd->ascnd", "abnst,abtnd->absnd")


def attend(queries, key_rows, value_rows, line):
    shape = queries.shape
    split = shape[:3] + (HEADS, HEAD_DIM)
    scores = jnp.einsum(
        score_forms[line],
        queries.reshape(split),
        key_rows.reshape(split),
        preferred_element_type=jnp.float32,
    ) * (1.0 / math.sqrt(HEAD_DIM))
    weights = jax.nn.softmax(scores, axis=-1).astype(jnp.bfloat16)
    mixed = jnp.einsum(
        mix_forms[line], weights, value_rows.reshape(split), preferred_element_type=jnp.float32
    )
    return mixed.astype(jnp.bfloat16).reshape(shape)


def full_block(state, gain, weight_in, weight_out, line):
    floats = state.astype(jnp.float32)
    meansq = jnp.mean(floats * floats, axis=-1, keepdims=True)
    normed = (floats * lax.rsqrt(meansq + EPS) * gain).astype(jnp.bfloat16)
    packed = jnp.dot(normed, weight_in, preferred_element_type=jnp.float32).astype(jnp.bfloat16)
    width = state.shape[-1]
    mixed = attend(
        packed[..., :width], packed[..., width : 2 * width], packed[..., 2 * width :], line
    )
    update = jnp.dot(mixed, weight_out, preferred_element_type=jnp.float32)
    return (floats + update).astype(jnp.bfloat16)


def general_body(video, norm_gain, qkv_weight, out_weight):
    state = full_block(video, norm_gain[0], qkv_weight[0], out_weight[0], 0)
    state = lax.all_to_all(state, "aa", split_axis=0, concat_axis=1, tiled=True)
    state = full_block(state, norm_gain[1], qkv_weight[1], out_weight[1], 1)
    state = lax.all_to_all(state, "ba", split_axis=1, concat_axis=2, tiled=True)
    state = full_block(state, norm_gain[2], qkv_weight[2], out_weight[2], 2)
    state = lax.all_to_all(state, "ba", split_axis=2, concat_axis=1, tiled=True)
    return lax.all_to_all(state, "aa", split_axis=1, concat_axis=0, tiled=True)


def normalise(floats, gain):
    meansq = jnp.mean(floats * floats, axis=-1, keepdims=True)
    return (floats * lax.rsqrt(meansq + EPS) * gain).astype(jnp.bfloat16)


def lane_halves(tokens):
    left = lax.broadcasted_iota(jnp.int32, (tokens, LANES), 1) < HEAD_DIM
    left = left.astype(jnp.float32)
    return left.astype(jnp.bfloat16), (1 - left).astype(jnp.bfloat16)


def tile_attention(packed, same_line, halves):
    tokens, width = packed.shape[0], packed.shape[1] // 3
    left, right = halves
    pieces = []
    for at in range(0, width, LANES):
        q = packed[:, at : at + LANES]
        k = packed[:, width + at : width + at + LANES]
        v = packed[:, 2 * width + at : 2 * width + at + LANES]
        scores = lax.dot_general(
            q,
            jnp.concatenate([k * left, k * right], axis=0),
            (((1,), (1,)), ((), ())),
            preferred_element_type=jnp.float32,
        )
        weights = []
        for head in range(2):
            own = jnp.where(same_line, scores[:, head * tokens : (head + 1) * tokens], HIDDEN)
            top = jnp.max(own, axis=-1, keepdims=True)
            weights.append(jnp.exp2(own - top).astype(jnp.bfloat16))
        values = jnp.concatenate(
            [
                jnp.concatenate([v * left, left], axis=1),
                jnp.concatenate([v * right, right], axis=1),
            ],
            axis=0,
        )
        mixed = jnp.dot(
            jnp.concatenate(weights, axis=1), values, preferred_element_type=jnp.float32
        )
        pieces.append((mixed[:, :LANES] / mixed[:, LANES:]).astype(jnp.bfloat16))
    return jnp.concatenate(pieces, axis=1)


def line_mask(tokens, line_of):
    rows = lax.broadcasted_iota(jnp.int32, (tokens, tokens), 0)
    columns = lax.broadcasted_iota(jnp.int32, (tokens, tokens), 1)
    return line_of(rows) == line_of(columns)


def project(normed, weight_ref, packed_ref, at):
    rows, width = normed.shape
    result = jnp.dot(normed, weight_ref[...], preferred_element_type=jnp.float32)
    scale = math.log2(math.e) / math.sqrt(HEAD_DIM)
    packed_ref[at : at + rows, :width] = (result[:, :width] * scale).astype(jnp.bfloat16)
    packed_ref[at : at + rows, width:] = result[:, width:].astype(jnp.bfloat16)


def lanes_of(value):
    return [value[:, at : at + LANES] for at in range(0, value.shape[1], LANES)]


def strided(ref, start, size, stride):
    return jnp.concatenate(
        [ref[at, pl.ds(start, size, stride=stride), :] for at in range(ref.shape[0])], axis=1
    )


def first_kernel(block, x_hbm, gain_hbm, win_hbm, wout_hbm, *rest):
    n = len(rest) - 9
    outs = rest[:n]
    win, wout, natural, lined, packed, mixed, sems, x_ref, gain_ref = rest[n:]
    frames, columns, width = x_ref.shape
    tokens = frames * columns
    loads = [
        pltpu.make_async_copy(source, target, sems.at[index])
        for index, (source, target) in enumerate(
            (
                (x_hbm, x_ref),
                (gain_hbm, gain_ref),
                (win_hbm.at[block], win),
                (wout_hbm.at[block], wout),
            )
        )
    ]
    for load in loads:
        load.start()
    loads[0].wait()
    loads[1].wait()
    for at, lanes in enumerate(lanes_of(x_ref[...].reshape(tokens, width).astype(jnp.float32))):
        natural[at] = lanes
    gain = gain_ref[block : block + 1]
    group = 256 // frames
    for column in range(0, columns, group):
        pieces = []
        for each in range(column, column + group):
            floats = strided(natural, each, frames, columns)
            for at, lanes in enumerate(lanes_of(floats)):
                lined[at, each * frames : (each + 1) * frames] = lanes
            pieces.append(normalise(floats, gain))
        if column == 0:
            loads[2].wait()
        project(jnp.concatenate(pieces, axis=0), win, packed, column * frames)
    mask = line_mask(LANES, lambda i: i // frames)
    halves = lane_halves(LANES)
    for at in range(0, tokens, LANES):
        mixed[at : at + LANES] = tile_attention(packed[at : at + LANES], mask, halves)
    loads[3].wait()
    for at in range(0, tokens, 256):
        update = jnp.dot(mixed[at : at + 256], wout[...], preferred_element_type=jnp.float32)
        for index, lanes in enumerate(lanes_of(update)):
            lined[index, at : at + 256] += lanes
    piece = frames // n
    spot = lax.axis_index("aa")
    for k in range(n):
        start = jnp.bitwise_xor(spot, k) * piece
        for frame in range(piece):
            outs[k][frame] = strided(lined, start + frame, columns, frames).astype(jnp.bfloat16)


def load_all(pairs, sems):
    loads = [
        pltpu.make_async_copy(source, target, sems.at[index])
        for index, (source, target) in enumerate(pairs)
    ]
    for load in loads:
        load.start()
    return loads


def prepare(refs, gain, win, packed_ref, at):
    pieces, start, count = [], at, 0
    for index, ref in enumerate(refs):
        floats = ref[...].reshape(-1, ref.shape[-1]).astype(jnp.float32)
        pieces.append(normalise(floats, gain))
        count += floats.shape[0]
        if count >= 256 or index == len(refs) - 1:
            normed = jnp.concatenate(pieces, axis=0) if len(pieces) > 1 else pieces[0]
            project(normed, win, packed_ref, start)
            pieces, start, count = [], start + count, 0


def weights_kernel(blocks, gain_hbm, win_hbm, wout_hbm, *rest):
    gain, copies, sems = rest[0], rest[1:-1], rest[-1]
    pairs = [(gain_hbm, gain)]
    for index, block in enumerate(blocks):
        pairs += [
            (win_hbm.at[block], copies[2 * index]),
            (wout_hbm.at[block], copies[2 * index + 1]),
        ]
    for load in load_all(pairs, sems):
        load.wait()


def group_kernel(block, count, *rest):
    ins, (gain_ref, win, packed) = rest[:count], rest[count:]
    prepare(ins, gain_ref[block : block + 1], win, packed, 0)


def share_rows(update, ins, keep, give):
    frames, columns, width = ins[0].shape
    per = frames * columns
    totals = [
        (ins[each][...].reshape(per, width).astype(jnp.float32) + update[each * per : (each + 1) * per])
        .astype(jnp.bfloat16)
        .reshape(frames, columns, width)
        for each in range(2)
    ]
    second = lax.axis_index("ba")

    @pl.when(second == 0)
    def _():
        keep[...] = totals[0]
        give[...] = totals[1]

    @pl.when(second != 0)
    def _():
        keep[...] = totals[1]
        give[...] = totals[0]


def middle_kernel(block, groups, pair, *rest):
    n = sum(map(len, groups))
    ins = rest[:n]
    ready = rest[n : n + len(groups) - 1]
    gain_ref, win, wout, mixed, keep_ref, give_ref, packed = rest[n + len(groups) - 1 :]
    frames, columns, _ = ins[0].shape
    per = columns * frames
    prepare([ins[k] for k in groups[-1]], gain_ref[block : block + 1], win, packed, 0)
    homes = [None] * n
    for group, ref in zip(groups, (*ready, packed)):
        for index, k in enumerate(group):
            homes[k] = (ref, index * per)
    share = LANES // n
    mask = line_mask(LANES, lambda i: i % share)
    halves = lane_halves(LANES)
    for at in range(0, per, share):
        tile = jnp.concatenate(
            [group[start + at : start + at + share] for group, start in homes], axis=0
        )
        result = tile_attention(tile, mask, halves)
        for k in range(n):
            mixed[k * per + at : k * per + at + share] = result[k * share : (k + 1) * share]
    k = 2 * pair
    update = jnp.dot(mixed[k * per : (k + 2) * per], wout[...], preferred_element_type=jnp.float32)
    share_rows(update, ins[k : k + 2], keep_ref.at[0], give_ref.at[0])


def middle_rest_kernel(pairs, mixed, wout, *rest):
    ins = rest[: 2 * len(pairs)]
    keep_ref, give_ref = rest[2 * len(pairs) :]
    frames, columns, _ = ins[0].shape
    per = columns * frames
    for index, pair in enumerate(pairs):
        k = 2 * pair
        update = jnp.dot(
            mixed[k * per : (k + 2) * per], wout[...], preferred_element_type=jnp.float32
        )
        share_rows(
            update,
            ins[2 * index : 2 * index + 2],
            keep_ref.at[index],
            give_ref.at[index],
        )


def kept_kernel(block, keep_ref, gain_ref, win, packed):
    prepare(
        [keep_ref.at[row] for row in range(keep_ref.shape[0])],
        gain_ref[block : block + 1],
        win,
        packed,
        0,
    )


def last_kernel(block, rows, keep_ref, got_ref, kept_packed, gain_ref, win, wout, *rest):
    outs = rest[: 2 * len(rows)]
    packed, mixed = rest[2 * len(rows) :]
    _, frames, columns, width = keep_ref.shape
    per = frames * columns
    tile = 2 * per
    gain = gain_ref[block : block + 1]
    prepare([got_ref.at[row] for row in rows], gain, win, packed, 0)
    mask = line_mask(LANES, lambda i: i // (2 * columns))
    halves = lane_halves(LANES)
    for index, row in enumerate(rows):
        for at in range(0, per, LANES // 2):
            strips = []
            for each in range(at, at + LANES // 2, columns):
                strips.append(kept_packed[row * per + each : row * per + each + columns])
                strips.append(packed[index * per + each : index * per + each + columns])
            start = index * tile + 2 * at
            mixed[start : start + LANES] = tile_attention(
                jnp.concatenate(strips, axis=0), mask, halves
            )
    for index, row in enumerate(rows):
        update = jnp.dot(
            mixed[index * tile : (index + 1) * tile],
            wout[...],
            preferred_element_type=jnp.float32,
        ).reshape(frames, 2 * columns, width)
        for half, ref in enumerate((keep_ref, got_ref)):
            outs[2 * index + half][...] = (
                ref[row].astype(jnp.float32) + update[:, half * columns : (half + 1) * columns]
            ).astype(jnp.bfloat16)


def join_kernel(senders, *rest):
    pieces, out, sems = rest[: len(senders)], rest[-2], rest[-1]
    size = pieces[0].shape[0]
    spot, core = lax.axis_index("aa"), lax.axis_index("ba")
    copies = []
    for index, (piece, (row, flip)) in enumerate(zip(pieces, senders)):
        sender = jnp.bitwise_xor(spot, 2 * row + jnp.bitwise_xor(core, flip))
        where = pl.ds(sender * size, size)
        copies.append(pltpu.make_async_copy(piece, out.at[where], sems.at[index]))
        copies[-1].start()
    for copy in copies:
        copy.wait()


VMEM = pl.BlockSpec(memory_space=pltpu.VMEM)
HBM = pl.BlockSpec(memory_space=pltpu.HBM)


def call(kernel, outs, in_specs, scratch_shapes, limit=8):
    return pl.pallas_call(
        kernel,
        out_shape=outs,
        in_specs=in_specs,
        out_specs=[VMEM] * len(outs),
        scratch_shapes=scratch_shapes,
        compiler_params=pltpu.CompilerParams(vmem_limit_bytes=limit << 20),
    )


def fast_body(n, video, norm_gain, qkv_weight, out_weight):
    frames, _, columns, width = video.shape
    piece = frames // n
    per = piece * columns
    tokens = frames * columns
    bf16, f32 = jnp.bfloat16, jnp.float32
    array = jax.ShapeDtypeStruct
    message = array((piece, columns, width), bf16)
    win_shape, wout_shape = (width, 3 * width), (width, width)
    gain_shape = norm_gain.shape
    local = pltpu.with_memory_space_constraint(
        video.reshape(frames, columns, width), pltpu.HBM
    )
    weights = tuple(
        pltpu.with_memory_space_constraint(w, pltpu.HBM)
        for w in (norm_gain, qkv_weight, out_weight)
    )

    sent = call(
        functools.partial(first_kernel, 0),
        [message] * n,
        [HBM] * 4,
        [
            pltpu.VMEM(win_shape, bf16),
            pltpu.VMEM(wout_shape, bf16),
            pltpu.VMEM((width // LANES, tokens, LANES), f32),
            pltpu.VMEM((width // LANES, tokens, LANES), f32),
            pltpu.VMEM((tokens, 3 * width), bf16),
            pltpu.VMEM((tokens, width), bf16),
            pltpu.SemaphoreType.DMA((4,)),
            pltpu.VMEM((frames, columns, width), bf16),
            pltpu.VMEM(gain_shape, f32),
        ],
        limit=24,
    )(local, *weights)

    came = {0: sent[0]}
    for k in range(1, n):
        came[k] = lax.ppermute(sent[k], "aa", [(i, i ^ k) for i in range(n)])

    later = range(1, norm_gain.shape[0])
    gain, *fetched = call(
        functools.partial(weights_kernel, later),
        [array(gain_shape, f32)] + [array(win_shape, bf16), array(wout_shape, bf16)] * len(later),
        [HBM] * 3,
        [pltpu.SemaphoreType.DMA((1 + 2 * len(later),))],
    )(*weights)
    win, wout, next_win, next_wout = fetched

    *groups, final = arrival_groups(n)
    ready = []
    for group in groups:
        ready += call(
            functools.partial(group_kernel, 1, len(group)),
            [array((len(group) * per, 3 * width), bf16)],
            [VMEM] * (len(group) + 2),
            [],
        )(*[came[k] for k in group], gain, win)

    lead, *others = (row for rows in row_plan(n) for row in rows)

    def kept(count):
        return array((count, piece, columns, width), bf16)

    mixed, keep, give = call(
        functools.partial(middle_kernel, 1, (*groups, final), lead),
        [array((tokens, width), bf16), kept(1), kept(1)],
        [VMEM] * (n + len(ready) + 3),
        [pltpu.VMEM((len(final) * per, 3 * width), bf16)],
    )(*[came[k] for k in range(n)], *ready, gain, win, wout)

    arrived, starts = [], []

    def swap(value):
        return lax.ppermute(value, "ba", [(0, 1), (1, 0)])

    def project_kept(value):
        count = value.shape[0]
        (packed,) = call(
            functools.partial(kept_kernel, 2),
            [array((count * per, 3 * width), bf16)],
            [VMEM] * 3,
            [],
        )(value, gain, next_win)
        return packed

    def finish(rows, pairs_of_rows, value, other, packed):
        results = call(
            functools.partial(last_kernel, 2, rows),
            [message] * (2 * len(rows)),
            [VMEM] * 6,
            [
                pltpu.VMEM((len(rows) * per, 3 * width), bf16),
                pltpu.VMEM((len(rows) * 2 * per, width), bf16),
            ],
        )(value, other, packed, gain, next_win, next_wout)
        for index, row in enumerate(pairs_of_rows):
            for flip in range(2):
                route = [
                    (2 * a + b, 2 * (a ^ (2 * row + b)) + (b ^ flip))
                    for a in range(n)
                    for b in range(2)
                ]
                arrived.append(lax.ppermute(results[2 * index + flip], ("aa", "ba"), route))
                starts.append((row, flip))

    got = swap(give)
    finish([0], [lead], keep, got, project_kept(keep))

    keep, give = call(
        functools.partial(middle_rest_kernel, others),
        [kept(len(others)), kept(len(others))],
        [VMEM] * (2 + 2 * len(others)),
        [],
    )(
        mixed,
        wout,
        *[came[2 * pair + each] for pair in others for each in range(2)],
    )
    got = swap(give)
    packed = project_kept(keep)
    for rows in row_plan(n)[1:]:
        finish([others.index(row) for row in rows], rows, keep, got, packed)

    def join(values, senders, base=None):
        count = len(values)
        given = [] if base is None else [base]
        return pl.pallas_call(
            functools.partial(join_kernel, senders),
            out_shape=array((frames, columns, width), bf16),
            in_specs=[VMEM] * count + [HBM] * len(given),
            out_specs=HBM,
            scratch_shapes=[pltpu.SemaphoreType.DMA((count,))],
            input_output_aliases={count: 0} if given else {},
            name="join",
            compiler_params=pltpu.CompilerParams(vmem_limit_bytes=4 << 20),
        )(*values, *given)

    out = join(arrived[:2], starts[:2])
    out = join(arrived[2:], starts[2:], out)
    return out.reshape(video.shape)


def body(n, cores, video, norm_gain, qkv_weight, out_weight):
    frames, rows, columns, width = video.shape
    piece = frames // n
    fast = (
        cores == 2
        and rows == 1
        and n % 4 == 0
        and n & (n - 1) == 0
        and LANES % n == 0
        and (LANES // n) % 16 == 0
        and frames % n == 0
        and LANES % frames == 0
        and frames % 8 == 0
        and columns % 16 == 0
        and LANES % (2 * columns) == 0
        and (columns * piece) % LANES == 0
        and (frames * columns) % 256 == 0
        and width == HEADS * HEAD_DIM
        and width % LANES == 0
    )
    if fast:
        return fast_body(n, video, norm_gain, qkv_weight, out_weight)
    return general_body(video, norm_gain, qkv_weight, out_weight)


def row_plan(n):
    half = n // 4
    return [[2 * half - 1], [*range(2 * half - 2, half - 1, -1), *range(half - 1, 0, -1)], [0]]


def arrival_groups(n):
    half, quarter = n // 2, n // 4
    return [
        [0, 1, *range(half, half + quarter)],
        [*range(2, half)],
        [*range(half + quarter, n - 1)],
        [n - 1],
    ]


def solution(mesh):
    n = mesh.shape["aa"]
    return jax.shard_map(
        functools.partial(body, n, mesh.shape["ba"]),
        mesh=mesh,
        in_specs=(P("groups", "aa", "ba", None), P(), P(), P()),
        out_specs=P("groups", "aa", "ba", None),
        check_vma=False,
    )
```

```python
import functools
import math

import jax
import jax.numpy as jnp
from jax import lax
from jax.experimental import pallas as pl
from jax.experimental.pallas import tpu as pltpu
from jax.sharding import PartitionSpec as P


HEADS = 8
HEAD_DIM = 64
EPS = 1e-06
LANES = 128
HIDDEN = -1e30


score_forms = ("sbcnd,tbcnd->bcnst", "ascnd,atcnd->acnst", "absnd,abtnd->abnst")
mix_forms = ("bcnst,tbcnd->sbcnd", "acnst,atcnd->ascnd", "abnst,abtnd->absnd")


def attend(queries, key_rows, value_rows, line):
    shape = queries.shape
    split = shape[:3] + (HEADS, HEAD_DIM)
    scores = jnp.einsum(
        score_forms[line],
        queries.reshape(split),
        key_rows.reshape(split),
        preferred_element_type=jnp.float32,
    ) * (1.0 / math.sqrt(HEAD_DIM))
    weights = jax.nn.softmax(scores, axis=-1).astype(jnp.bfloat16)
    mixed = jnp.einsum(
        mix_forms[line], weights, value_rows.reshape(split), preferred_element_type=jnp.float32
    )
    return mixed.astype(jnp.bfloat16).reshape(shape)


def full_block(state, gain, weight_in, weight_out, line):
    floats = state.astype(jnp.float32)
    meansq = jnp.mean(floats * floats, axis=-1, keepdims=True)
    normed = (floats * lax.rsqrt(meansq + EPS) * gain).astype(jnp.bfloat16)
    packed = jnp.dot(normed, weight_in, preferred_element_type=jnp.float32).astype(jnp.bfloat16)
    width = state.shape[-1]
    mixed = attend(
        packed[..., :width], packed[..., width : 2 * width], packed[..., 2 * width :], line
    )
    update = jnp.dot(mixed, weight_out, preferred_element_type=jnp.float32)
    return (floats + update).astype(jnp.bfloat16)


def general_body(video, norm_gain, qkv_weight, out_weight):
    state = full_block(video, norm_gain[0], qkv_weight[0], out_weight[0], 0)
    state = lax.all_to_all(state, "aa", split_axis=0, concat_axis=1, tiled=True)
    state = full_block(state, norm_gain[1], qkv_weight[1], out_weight[1], 1)
    state = lax.all_to_all(state, "ba", split_axis=1, concat_axis=2, tiled=True)
    state = full_block(state, norm_gain[2], qkv_weight[2], out_weight[2], 2)
    state = lax.all_to_all(state, "ba", split_axis=2, concat_axis=1, tiled=True)
    return lax.all_to_all(state, "aa", split_axis=1, concat_axis=0, tiled=True)


def normalise(floats, gain):
    meansq = jnp.mean(floats * floats, axis=-1, keepdims=True)
    return (floats * lax.rsqrt(meansq + EPS) * gain).astype(jnp.bfloat16)


def lane_halves(tokens):
    left = lax.broadcasted_iota(jnp.int32, (tokens, LANES), 1) < HEAD_DIM
    left = left.astype(jnp.float32)
    return left.astype(jnp.bfloat16), (1 - left).astype(jnp.bfloat16)


def tile_attention(packed, same_line, halves):
    tokens, width = packed.shape[0], packed.shape[1] // 3
    left, right = halves
    pieces = []
    for at in range(0, width, LANES):
        q = packed[:, at : at + LANES]
        k = packed[:, width + at : width + at + LANES]
        v = packed[:, 2 * width + at : 2 * width + at + LANES]
        scores = lax.dot_general(
            q,
            jnp.concatenate([k * left, k * right], axis=0),
            (((1,), (1,)), ((), ())),
            preferred_element_type=jnp.float32,
        )
        weights = []
        for head in range(2):
            own = jnp.where(same_line, scores[:, head * tokens : (head + 1) * tokens], HIDDEN)
            top = jnp.max(own, axis=-1, keepdims=True)
            weights.append(jnp.exp2(own - top).astype(jnp.bfloat16))
        values = jnp.concatenate(
            [
                jnp.concatenate([v * left, left], axis=1),
                jnp.concatenate([v * right, right], axis=1),
            ],
            axis=0,
        )
        mixed = jnp.dot(
            jnp.concatenate(weights, axis=1), values, preferred_element_type=jnp.float32
        )
        pieces.append((mixed[:, :LANES] / mixed[:, LANES:]).astype(jnp.bfloat16))
    return jnp.concatenate(pieces, axis=1)


def line_mask(tokens, line_of):
    rows = lax.broadcasted_iota(jnp.int32, (tokens, tokens), 0)
    columns = lax.broadcasted_iota(jnp.int32, (tokens, tokens), 1)
    return line_of(rows) == line_of(columns)


def project(normed, weight_ref, packed_ref, at):
    rows, width = normed.shape
    result = jnp.dot(normed, weight_ref[...], preferred_element_type=jnp.float32)
    scale = math.log2(math.e) / math.sqrt(HEAD_DIM)
    packed_ref[at : at + rows, :width] = (result[:, :width] * scale).astype(jnp.bfloat16)
    packed_ref[at : at + rows, width:] = result[:, width:].astype(jnp.bfloat16)


def lanes_of(value):
    return [value[:, at : at + LANES] for at in range(0, value.shape[1], LANES)]


def strided(ref, start, size, stride):
    return jnp.concatenate(
        [ref[at, pl.ds(start, size, stride=stride), :] for at in range(ref.shape[0])], axis=1
    )


def first_kernel(block, x_hbm, gain_hbm, win_hbm, wout_hbm, *rest):
    n = len(rest) - 9
    outs = rest[:n]
    win, wout, natural, lined, packed, mixed, sems, x_ref, gain_ref = rest[n:]
    parts, frames, cut, width = x_ref.shape
    columns = parts * cut
    tokens = frames * columns
    loads = load_all(
        (
            *((x_hbm.at[:, pl.ds(part * cut, cut)], x_ref.at[part]) for part in range(parts)),
            (gain_hbm, gain_ref),
            (win_hbm.at[block], win),
            (wout_hbm.at[block], wout),
        ),
        sems,
    )
    loads[parts].wait()
    gain = gain_ref[block : block + 1]
    group = 256 // frames
    for part in range(parts):
        loads[part].wait()
        floats = x_ref[part].reshape(frames * cut, width).astype(jnp.float32)
        for at, lanes in enumerate(lanes_of(floats)):
            natural[part * (width // LANES) + at] = lanes
        mine = natural.at[pl.ds(part * (width // LANES), width // LANES)]
        normed = []
        for column in range(part * cut, (part + 1) * cut):
            floats = strided(mine, column % cut, frames, cut)
            for at, lanes in enumerate(lanes_of(floats)):
                lined[at, column * frames : (column + 1) * frames] = lanes
            normed.append(normalise(floats, gain))
        if part == 0:
            loads[parts + 1].wait()
        for at in range(0, cut, group):
            project(
                jnp.concatenate(normed[at : at + group], axis=0),
                win,
                packed,
                (part * cut + at) * frames,
            )
    mask = line_mask(LANES, lambda i: i // frames)
    halves = lane_halves(LANES)
    for at in range(0, tokens, LANES):
        mixed[at : at + LANES] = tile_attention(packed[at : at + LANES], mask, halves)
    loads[parts + 2].wait()
    for at in range(0, tokens, 256):
        update = jnp.dot(mixed[at : at + 256], wout[...], preferred_element_type=jnp.float32)
        for index, lanes in enumerate(lanes_of(update)):
            lined[index, at : at + 256] += lanes
    piece = frames // n
    spot = lax.axis_index("aa")
    for k in range(n):
        start = jnp.bitwise_xor(spot, k) * piece
        for frame in range(piece):
            outs[k][frame] = strided(lined, start + frame, columns, frames).astype(jnp.bfloat16)


def load_all(pairs, sems):
    loads = [
        pltpu.make_async_copy(source, target, sems.at[index])
        for index, (source, target) in enumerate(pairs)
    ]
    for load in loads:
        load.start()
    return loads


def prepare(refs, gain, win, packed_ref, at):
    pieces, start, count = [], at, 0
    for index, ref in enumerate(refs):
        floats = ref[...].reshape(-1, ref.shape[-1]).astype(jnp.float32)
        pieces.append(normalise(floats, gain))
        count += floats.shape[0]
        if count >= 256 or index == len(refs) - 1:
            normed = jnp.concatenate(pieces, axis=0) if len(pieces) > 1 else pieces[0]
            project(normed, win, packed_ref, start)
            pieces, start, count = [], start + count, 0


def weights_kernel(blocks, gain_hbm, win_hbm, wout_hbm, *rest):
    gain, copies, sems = rest[0], rest[1:-1], rest[-1]
    pairs = [(gain_hbm, gain)]
    for index, block in enumerate(blocks):
        pairs += [
            (win_hbm.at[block], copies[2 * index]),
            (wout_hbm.at[block], copies[2 * index + 1]),
        ]
    for load in load_all(pairs, sems):
        load.wait()


def group_kernel(block, count, *rest):
    ins, (gain_ref, win, packed) = rest[:count], rest[count:]
    prepare(ins, gain_ref[block : block + 1], win, packed, 0)


def share_rows(update, ins, keep, give):
    frames, columns, width = ins[0].shape
    per = frames * columns
    totals = [
        (ins[each][...].reshape(per, width).astype(jnp.float32) + update[each * per : (each + 1) * per])
        .astype(jnp.bfloat16)
        .reshape(frames, columns, width)
        for each in range(2)
    ]
    second = lax.axis_index("ba")

    @pl.when(second == 0)
    def _():
        keep[...] = totals[0]
        give[...] = totals[1]

    @pl.when(second != 0)
    def _():
        keep[...] = totals[1]
        give[...] = totals[0]


def middle_kernel(block, groups, pair, *rest):
    n = sum(map(len, groups))
    ins = rest[:n]
    ready = rest[n : n + len(groups) - 1]
    gain_ref, win, wout, mixed, keep_ref, give_ref, packed = rest[n + len(groups) - 1 :]
    frames, columns, _ = ins[0].shape
    per = columns * frames
    prepare([ins[k] for k in groups[-1]], gain_ref[block : block + 1], win, packed, 0)
    homes = [None] * n
    for group, ref in zip(groups, (*ready, packed)):
        for index, k in enumerate(group):
            homes[k] = (ref, index * per)
    share = LANES // n
    mask = line_mask(LANES, lambda i: i % share)
    halves = lane_halves(LANES)
    for at in range(0, per, share):
        tile = jnp.concatenate(
            [group[start + at : start + at + share] for group, start in homes], axis=0
        )
        result = tile_attention(tile, mask, halves)
        for k in range(n):
            mixed[k * per + at : k * per + at + share] = result[k * share : (k + 1) * share]
    k = 2 * pair
    update = jnp.dot(mixed[k * per : (k + 2) * per], wout[...], preferred_element_type=jnp.float32)
    share_rows(update, ins[k : k + 2], keep_ref.at[0], give_ref.at[0])


def middle_rest_kernel(pairs, mixed, wout, *rest):
    ins = rest[: 2 * len(pairs)]
    keep_ref, give_ref = rest[2 * len(pairs) :]
    frames, columns, _ = ins[0].shape
    per = columns * frames
    for index, pair in enumerate(pairs):
        k = 2 * pair
        update = jnp.dot(
            mixed[k * per : (k + 2) * per], wout[...], preferred_element_type=jnp.float32
        )
        share_rows(
            update,
            ins[2 * index : 2 * index + 2],
            keep_ref.at[index],
            give_ref.at[index],
        )


def kept_kernel(block, keep_ref, gain_ref, win, packed):
    prepare(
        [keep_ref.at[row] for row in range(keep_ref.shape[0])],
        gain_ref[block : block + 1],
        win,
        packed,
        0,
    )


def last_kernel(block, rows, keep_ref, got_ref, kept_packed, gain_ref, win, wout, *rest):
    outs = rest[: 2 * len(rows)]
    packed, mixed = rest[2 * len(rows) :]
    _, frames, columns, width = keep_ref.shape
    per = frames * columns
    tile = 2 * per
    gain = gain_ref[block : block + 1]
    prepare([got_ref.at[row] for row in rows], gain, win, packed, 0)
    mask = line_mask(LANES, lambda i: i // (2 * columns))
    halves = lane_halves(LANES)
    for index, row in enumerate(rows):
        for at in range(0, per, LANES // 2):
            strips = []
            for each in range(at, at + LANES // 2, columns):
                strips.append(kept_packed[row * per + each : row * per + each + columns])
                strips.append(packed[index * per + each : index * per + each + columns])
            start = index * tile + 2 * at
            mixed[start : start + LANES] = tile_attention(
                jnp.concatenate(strips, axis=0), mask, halves
            )
    for index, row in enumerate(rows):
        update = jnp.dot(
            mixed[index * tile : (index + 1) * tile],
            wout[...],
            preferred_element_type=jnp.float32,
        ).reshape(frames, 2 * columns, width)
        for half, ref in enumerate((keep_ref, got_ref)):
            outs[2 * index + half][...] = (
                ref[row].astype(jnp.float32) + update[:, half * columns : (half + 1) * columns]
            ).astype(jnp.bfloat16)


def join_kernel(senders, *rest):
    pieces, out, sems = rest[: len(senders)], rest[-2], rest[-1]
    size = pieces[0].shape[0]
    spot, core = lax.axis_index("aa"), lax.axis_index("ba")
    copies = []
    for index, (piece, (row, flip)) in enumerate(zip(pieces, senders)):
        sender = jnp.bitwise_xor(spot, 2 * row + jnp.bitwise_xor(core, flip))
        where = pl.ds(sender * size, size)
        copies.append(pltpu.make_async_copy(piece, out.at[where], sems.at[index]))
        copies[-1].start()
    for copy in copies:
        copy.wait()


VMEM = pl.BlockSpec(memory_space=pltpu.VMEM)
HBM = pl.BlockSpec(memory_space=pltpu.HBM)


def call(kernel, outs, in_specs, scratch_shapes, limit=8):
    return pl.pallas_call(
        kernel,
        out_shape=outs,
        in_specs=in_specs,
        out_specs=[VMEM] * len(outs),
        scratch_shapes=scratch_shapes,
        compiler_params=pltpu.CompilerParams(vmem_limit_bytes=limit << 20),
    )


def fast_body(n, video, norm_gain, qkv_weight, out_weight):
    frames, _, columns, width = video.shape
    piece = frames // n
    per = piece * columns
    tokens = frames * columns
    bf16, f32 = jnp.bfloat16, jnp.float32
    array = jax.ShapeDtypeStruct
    message = array((piece, columns, width), bf16)
    win_shape, wout_shape = (width, 3 * width), (width, width)
    gain_shape = norm_gain.shape
    local = pltpu.with_memory_space_constraint(
        video.reshape(frames, columns, width), pltpu.HBM
    )
    weights = tuple(
        pltpu.with_memory_space_constraint(w, pltpu.HBM)
        for w in (norm_gain, qkv_weight, out_weight)
    )

    sent = call(
        functools.partial(first_kernel, 0),
        [message] * n,
        [HBM] * 4,
        [
            pltpu.VMEM(win_shape, bf16),
            pltpu.VMEM(wout_shape, bf16),
            pltpu.VMEM((2 * width // LANES, tokens // 2, LANES), f32),
            pltpu.VMEM((width // LANES, tokens, LANES), f32),
            pltpu.VMEM((tokens, 3 * width), bf16),
            pltpu.VMEM((tokens, width), bf16),
            pltpu.SemaphoreType.DMA((5,)),
            pltpu.VMEM((2, frames, columns // 2, width), bf16),
            pltpu.VMEM(gain_shape, f32),
        ],
        limit=24,
    )(local, *weights)

    came = {0: sent[0]}
    for k in range(1, n):
        came[k] = lax.ppermute(sent[k], "aa", [(i, i ^ k) for i in range(n)])

    later = range(1, norm_gain.shape[0])
    gain, *fetched = call(
        functools.partial(weights_kernel, later),
        [array(gain_shape, f32)] + [array(win_shape, bf16), array(wout_shape, bf16)] * len(later),
        [HBM] * 3,
        [pltpu.SemaphoreType.DMA((1 + 2 * len(later),))],
    )(*weights)
    win, wout, next_win, next_wout = fetched

    *groups, final = arrival_groups(n)
    ready = []
    for group in groups:
        ready += call(
            functools.partial(group_kernel, 1, len(group)),
            [array((len(group) * per, 3 * width), bf16)],
            [VMEM] * (len(group) + 2),
            [],
        )(*[came[k] for k in group], gain, win)

    lead, *others = (row for rows in row_plan(n) for row in rows)

    def kept(count):
        return array((count, piece, columns, width), bf16)

    mixed, keep, give = call(
        functools.partial(middle_kernel, 1, (*groups, final), lead),
        [array((tokens, width), bf16), kept(1), kept(1)],
        [VMEM] * (n + len(ready) + 3),
        [pltpu.VMEM((len(final) * per, 3 * width), bf16)],
    )(*[came[k] for k in range(n)], *ready, gain, win, wout)

    arrived, starts = [], []

    def swap(value):
        return lax.ppermute(value, "ba", [(0, 1), (1, 0)])

    def project_kept(value):
        count = value.shape[0]
        (packed,) = call(
            functools.partial(kept_kernel, 2),
            [array((count * per, 3 * width), bf16)],
            [VMEM] * 3,
            [],
        )(value, gain, next_win)
        return packed

    def finish(rows, pairs_of_rows, value, other, packed):
        results = call(
            functools.partial(last_kernel, 2, rows),
            [message] * (2 * len(rows)),
            [VMEM] * 6,
            [
                pltpu.VMEM((len(rows) * per, 3 * width), bf16),
                pltpu.VMEM((len(rows) * 2 * per, width), bf16),
            ],
        )(value, other, packed, gain, next_win, next_wout)
        for index, row in enumerate(pairs_of_rows):
            for flip in range(2):
                route = [
                    (2 * a + b, 2 * (a ^ (2 * row + b)) + (b ^ flip))
                    for a in range(n)
                    for b in range(2)
                ]
                arrived.append(lax.ppermute(results[2 * index + flip], ("aa", "ba"), route))
                starts.append((row, flip))

    got = swap(give)
    finish([0], [lead], keep, got, project_kept(keep))

    keep, give = call(
        functools.partial(middle_rest_kernel, others),
        [kept(len(others)), kept(len(others))],
        [VMEM] * (2 + 2 * len(others)),
        [],
    )(
        mixed,
        wout,
        *[came[2 * pair + each] for pair in others for each in range(2)],
    )
    got = swap(give)
    packed = project_kept(keep)
    for rows in row_plan(n)[1:]:
        finish([others.index(row) for row in rows], rows, keep, got, packed)

    def join(values, senders, base=None):
        count = len(values)
        given = [] if base is None else [base]
        return pl.pallas_call(
            functools.partial(join_kernel, senders),
            out_shape=array((frames, columns, width), bf16),
            in_specs=[VMEM] * count + [HBM] * len(given),
            out_specs=HBM,
            scratch_shapes=[pltpu.SemaphoreType.DMA((count,))],
            input_output_aliases={count: 0} if given else {},
            name="join",
            compiler_params=pltpu.CompilerParams(vmem_limit_bytes=4 << 20),
        )(*values, *given)

    slow = [index for index, (row, _) in enumerate(starts) if row == others[0]]
    soon = [index for index in range(n) if index not in slow]
    out = join([arrived[index] for index in soon], [starts[index] for index in soon])
    out = join([arrived[index] for index in slow], [starts[index] for index in slow], out)
    return out.reshape(video.shape)


def body(n, cores, video, norm_gain, qkv_weight, out_weight):
    frames, rows, columns, width = video.shape
    piece = frames // n
    fast = (
        cores == 2
        and rows == 1
        and n % 4 == 0
        and n & (n - 1) == 0
        and LANES % n == 0
        and (LANES // n) % 16 == 0
        and frames % n == 0
        and LANES % frames == 0
        and frames % 8 == 0
        and columns % 16 == 0
        and LANES % (2 * columns) == 0
        and (columns * piece) % LANES == 0
        and (frames * columns) % 256 == 0
        and width == HEADS * HEAD_DIM
        and width % LANES == 0
    )
    if fast:
        return fast_body(n, video, norm_gain, qkv_weight, out_weight)
    return general_body(video, norm_gain, qkv_weight, out_weight)


def row_plan(n):
    half = n // 4
    return [[2 * half - 1], [*range(2 * half - 2, half - 1, -1), *range(half - 1, 0, -1)], [0]]


def arrival_groups(n):
    half, quarter = n // 2, n // 4
    return [
        [0, 1, *range(half, half + quarter)],
        [*range(2, half)],
        [*range(half + quarter, n - 1)],
        [n - 1],
    ]


def solution(mesh):
    n = mesh.shape["aa"]
    return jax.shard_map(
        functools.partial(body, n, mesh.shape["ba"]),
        mesh=mesh,
        in_specs=(P("groups", "aa", "ba", None), P(), P(), P()),
        out_specs=P("groups", "aa", "ba", None),
        check_vma=False,
    )
```

```python
import functools
import math

import jax
import jax.numpy as jnp
from jax import lax
from jax.experimental import pallas as pl
from jax.experimental.pallas import tpu as pltpu
from jax.sharding import PartitionSpec as P


HEADS = 8
HEAD_DIM = 64
EPS = 1e-06
LANES = 128
HIDDEN = -1e30


score_forms = ("sbcnd,tbcnd->bcnst", "ascnd,atcnd->acnst", "absnd,abtnd->abnst")
mix_forms = ("bcnst,tbcnd->sbcnd", "acnst,atcnd->ascnd", "abnst,abtnd->absnd")


def attend(queries, key_rows, value_rows, line):
    shape = queries.shape
    split = shape[:3] + (HEADS, HEAD_DIM)
    scores = jnp.einsum(
        score_forms[line],
        queries.reshape(split),
        key_rows.reshape(split),
        preferred_element_type=jnp.float32,
    ) * (1.0 / math.sqrt(HEAD_DIM))
    weights = jax.nn.softmax(scores, axis=-1).astype(jnp.bfloat16)
    mixed = jnp.einsum(
        mix_forms[line], weights, value_rows.reshape(split), preferred_element_type=jnp.float32
    )
    return mixed.astype(jnp.bfloat16).reshape(shape)


def full_block(state, gain, weight_in, weight_out, line):
    floats = state.astype(jnp.float32)
    meansq = jnp.mean(floats * floats, axis=-1, keepdims=True)
    normed = (floats * lax.rsqrt(meansq + EPS) * gain).astype(jnp.bfloat16)
    packed = jnp.dot(normed, weight_in, preferred_element_type=jnp.float32).astype(jnp.bfloat16)
    width = state.shape[-1]
    mixed = attend(
        packed[..., :width], packed[..., width : 2 * width], packed[..., 2 * width :], line
    )
    update = jnp.dot(mixed, weight_out, preferred_element_type=jnp.float32)
    return (floats + update).astype(jnp.bfloat16)


def general_body(video, norm_gain, qkv_weight, out_weight):
    state = full_block(video, norm_gain[0], qkv_weight[0], out_weight[0], 0)
    state = lax.all_to_all(state, "aa", split_axis=0, concat_axis=1, tiled=True)
    state = full_block(state, norm_gain[1], qkv_weight[1], out_weight[1], 1)
    state = lax.all_to_all(state, "ba", split_axis=1, concat_axis=2, tiled=True)
    state = full_block(state, norm_gain[2], qkv_weight[2], out_weight[2], 2)
    state = lax.all_to_all(state, "ba", split_axis=2, concat_axis=1, tiled=True)
    return lax.all_to_all(state, "aa", split_axis=1, concat_axis=0, tiled=True)


def normalise(floats, gain):
    meansq = jnp.mean(floats * floats, axis=-1, keepdims=True)
    return (floats * lax.rsqrt(meansq + EPS) * gain).astype(jnp.bfloat16)


def lane_halves(tokens):
    left = lax.broadcasted_iota(jnp.int32, (tokens, LANES), 1) < HEAD_DIM
    left = left.astype(jnp.float32)
    return left.astype(jnp.bfloat16), (1 - left).astype(jnp.bfloat16)


def tile_attention(packed, same_line, halves):
    tokens, width = packed.shape[0], packed.shape[1] // 3
    left, right = halves
    scale = math.log2(math.e) / math.sqrt(HEAD_DIM)
    pieces = []
    for at in range(0, width, LANES):
        q = packed[:, at : at + LANES]
        k = packed[:, width + at : width + at + LANES]
        v = packed[:, 2 * width + at : 2 * width + at + LANES]
        scores = lax.dot_general(
            q,
            jnp.concatenate([k * left, k * right], axis=0),
            (((1,), (1,)), ((), ())),
            preferred_element_type=jnp.float32,
        )
        weights = []
        for head in range(2):
            own = jnp.where(same_line, scores[:, head * tokens : (head + 1) * tokens], HIDDEN)
            top = jnp.max(own, axis=-1, keepdims=True)
            weights.append(jnp.exp2((own - top) * scale).astype(jnp.bfloat16))
        values = jnp.concatenate(
            [
                jnp.concatenate([v * left, left], axis=1),
                jnp.concatenate([v * right, right], axis=1),
            ],
            axis=0,
        )
        mixed = jnp.dot(
            jnp.concatenate(weights, axis=1), values, preferred_element_type=jnp.float32
        )
        pieces.append((mixed[:, :LANES] / mixed[:, LANES:]).astype(jnp.bfloat16))
    return jnp.concatenate(pieces, axis=1)


def line_mask(tokens, line_of):
    rows = lax.broadcasted_iota(jnp.int32, (tokens, tokens), 0)
    columns = lax.broadcasted_iota(jnp.int32, (tokens, tokens), 1)
    return line_of(rows) == line_of(columns)


def project(normed, weight_ref, packed_ref, at):
    packed_ref[at : at + normed.shape[0]] = jnp.dot(
        normed, weight_ref[...], preferred_element_type=jnp.float32
    ).astype(jnp.bfloat16)


def lanes_of(value):
    return [value[:, at : at + LANES] for at in range(0, value.shape[1], LANES)]


def strided(ref, start, size, stride):
    return jnp.concatenate(
        [ref[at, pl.ds(start, size, stride=stride), :] for at in range(ref.shape[0])], axis=1
    )


def first_kernel(block, x_hbm, gain_hbm, win_hbm, wout_hbm, *rest):
    n = len(rest) - 9
    outs = rest[:n]
    win, wout, natural, lined, packed, mixed, sems, x_ref, gain_ref = rest[n:]
    parts, frames, cut, width = x_ref.shape
    columns = parts * cut
    tokens = frames * columns
    loads = load_all(
        (
            *((x_hbm.at[:, pl.ds(part * cut, cut)], x_ref.at[part]) for part in range(parts)),
            (gain_hbm, gain_ref),
            (win_hbm.at[block], win),
            (wout_hbm.at[block], wout),
        ),
        sems,
    )
    loads[parts].wait()
    gain = gain_ref[block : block + 1]
    group = 256 // frames
    for part in range(parts):
        loads[part].wait()
        floats = x_ref[part].reshape(frames * cut, width).astype(jnp.float32)
        for at, lanes in enumerate(lanes_of(floats)):
            natural[part * (width // LANES) + at] = lanes
        mine = natural.at[pl.ds(part * (width // LANES), width // LANES)]
        normed = []
        for column in range(part * cut, (part + 1) * cut):
            floats = strided(mine, column % cut, frames, cut)
            for at, lanes in enumerate(lanes_of(floats)):
                lined[at, column * frames : (column + 1) * frames] = lanes
            normed.append(normalise(floats, gain))
        if part == 0:
            loads[parts + 1].wait()
        for at in range(0, cut, group):
            project(
                jnp.concatenate(normed[at : at + group], axis=0),
                win,
                packed,
                (part * cut + at) * frames,
            )
    mask = line_mask(LANES, lambda i: i // frames)
    halves = lane_halves(LANES)
    for at in range(0, tokens, LANES):
        mixed[at : at + LANES] = tile_attention(packed[at : at + LANES], mask, halves)
    loads[parts + 2].wait()
    for at in range(0, tokens, 256):
        update = jnp.dot(mixed[at : at + 256], wout[...], preferred_element_type=jnp.float32)
        for index, lanes in enumerate(lanes_of(update)):
            lined[index, at : at + 256] += lanes
    piece = frames // n
    spot = lax.axis_index("aa")
    for k in range(n):
        start = jnp.bitwise_xor(spot, k) * piece
        for frame in range(piece):
            outs[k][frame] = strided(lined, start + frame, columns, frames).astype(jnp.bfloat16)


def load_all(pairs, sems):
    loads = [
        pltpu.make_async_copy(source, target, sems.at[index])
        for index, (source, target) in enumerate(pairs)
    ]
    for load in loads:
        load.start()
    return loads


def prepare(refs, gain, win, packed_ref, at):
    pieces, start, count = [], at, 0
    for index, ref in enumerate(refs):
        floats = ref[...].reshape(-1, ref.shape[-1]).astype(jnp.float32)
        pieces.append(normalise(floats, gain))
        count += floats.shape[0]
        if count >= 256 or index == len(refs) - 1:
            normed = jnp.concatenate(pieces, axis=0) if len(pieces) > 1 else pieces[0]
            project(normed, win, packed_ref, start)
            pieces, start, count = [], start + count, 0


def weights_kernel(blocks, gain_hbm, win_hbm, wout_hbm, *rest):
    gain, copies, sems = rest[0], rest[1:-1], rest[-1]
    pairs = [(gain_hbm, gain)]
    for index, block in enumerate(blocks):
        pairs += [
            (win_hbm.at[block], copies[2 * index]),
            (wout_hbm.at[block], copies[2 * index + 1]),
        ]
    for load in load_all(pairs, sems):
        load.wait()


def group_kernel(block, count, *rest):
    ins, (gain_ref, win, packed) = rest[:count], rest[count:]
    prepare(ins, gain_ref[block : block + 1], win, packed, 0)


def share_rows(update, ins, keep, give):
    frames, columns, width = ins[0].shape
    per = frames * columns
    totals = [
        (ins[each][...].reshape(per, width).astype(jnp.float32) + update[each * per : (each + 1) * per])
        .astype(jnp.bfloat16)
        .reshape(frames, columns, width)
        for each in range(2)
    ]
    second = lax.axis_index("ba")

    @pl.when(second == 0)
    def _():
        keep[...] = totals[0]
        give[...] = totals[1]

    @pl.when(second != 0)
    def _():
        keep[...] = totals[1]
        give[...] = totals[0]


def middle_kernel(block, groups, pair, *rest):
    n = sum(map(len, groups))
    ins = rest[:n]
    ready = rest[n : n + len(groups) - 1]
    gain_ref, win, wout, mixed, keep_ref, give_ref, packed = rest[n + len(groups) - 1 :]
    frames, columns, _ = ins[0].shape
    per = columns * frames
    prepare([ins[k] for k in groups[-1]], gain_ref[block : block + 1], win, packed, 0)
    homes = [None] * n
    for group, ref in zip(groups, (*ready, packed)):
        for index, k in enumerate(group):
            homes[k] = (ref, index * per)
    share = LANES // n
    mask = line_mask(LANES, lambda i: i % share)
    halves = lane_halves(LANES)
    for at in range(0, per, share):
        tile = jnp.concatenate(
            [group[start + at : start + at + share] for group, start in homes], axis=0
        )
        result = tile_attention(tile, mask, halves)
        for k in range(n):
            mixed[k * per + at : k * per + at + share] = result[k * share : (k + 1) * share]
    k = 2 * pair
    update = jnp.dot(mixed[k * per : (k + 2) * per], wout[...], preferred_element_type=jnp.float32)
    share_rows(update, ins[k : k + 2], keep_ref.at[0], give_ref.at[0])


def middle_rest_kernel(pairs, mixed, wout, *rest):
    ins = rest[: 2 * len(pairs)]
    keep_ref, give_ref = rest[2 * len(pairs) :]
    frames, columns, _ = ins[0].shape
    per = columns * frames
    for index, pair in enumerate(pairs):
        k = 2 * pair
        update = jnp.dot(
            mixed[k * per : (k + 2) * per], wout[...], preferred_element_type=jnp.float32
        )
        share_rows(
            update,
            ins[2 * index : 2 * index + 2],
            keep_ref.at[index],
            give_ref.at[index],
        )


def kept_kernel(block, keep_ref, gain_ref, win, packed):
    prepare(
        [keep_ref.at[row] for row in range(keep_ref.shape[0])],
        gain_ref[block : block + 1],
        win,
        packed,
        0,
    )


def last_kernel(block, rows, keep_ref, got_ref, kept_packed, gain_ref, win, wout, *rest):
    outs = rest[: 2 * len(rows)]
    packed, mixed = rest[2 * len(rows) :]
    _, frames, columns, width = keep_ref.shape
    per = frames * columns
    tile = 2 * per
    gain = gain_ref[block : block + 1]
    prepare([got_ref.at[row] for row in rows], gain, win, packed, 0)
    mask = line_mask(LANES, lambda i: i // (2 * columns))
    halves = lane_halves(LANES)
    for index, row in enumerate(rows):
        for at in range(0, per, LANES // 2):
            strips = []
            for each in range(at, at + LANES // 2, columns):
                strips.append(kept_packed[row * per + each : row * per + each + columns])
                strips.append(packed[index * per + each : index * per + each + columns])
            start = index * tile + 2 * at
            mixed[start : start + LANES] = tile_attention(
                jnp.concatenate(strips, axis=0), mask, halves
            )
    for index, row in enumerate(rows):
        update = jnp.dot(
            mixed[index * tile : (index + 1) * tile],
            wout[...],
            preferred_element_type=jnp.float32,
        ).reshape(frames, 2 * columns, width)
        for half, ref in enumerate((keep_ref, got_ref)):
            outs[2 * index + half][...] = (
                ref[row].astype(jnp.float32) + update[:, half * columns : (half + 1) * columns]
            ).astype(jnp.bfloat16)


def join_kernel(senders, *rest):
    pieces, out, sems = rest[: len(senders)], rest[-2], rest[-1]
    size = pieces[0].shape[0]
    spot, core = lax.axis_index("aa"), lax.axis_index("ba")
    copies = []
    for index, (piece, (row, flip)) in enumerate(zip(pieces, senders)):
        sender = jnp.bitwise_xor(spot, 2 * row + jnp.bitwise_xor(core, flip))
        where = pl.ds(sender * size, size)
        copies.append(pltpu.make_async_copy(piece, out.at[where], sems.at[index]))
        copies[-1].start()
    for copy in copies:
        copy.wait()


VMEM = pl.BlockSpec(memory_space=pltpu.VMEM)
HBM = pl.BlockSpec(memory_space=pltpu.HBM)


def call(kernel, outs, in_specs, scratch_shapes, limit=8):
    return pl.pallas_call(
        kernel,
        out_shape=outs,
        in_specs=in_specs,
        out_specs=[VMEM] * len(outs),
        scratch_shapes=scratch_shapes,
        compiler_params=pltpu.CompilerParams(vmem_limit_bytes=limit << 20),
    )


def fast_body(n, video, norm_gain, qkv_weight, out_weight):
    frames, _, columns, width = video.shape
    piece = frames // n
    per = piece * columns
    tokens = frames * columns
    bf16, f32 = jnp.bfloat16, jnp.float32
    array = jax.ShapeDtypeStruct
    message = array((piece, columns, width), bf16)
    win_shape, wout_shape = (width, 3 * width), (width, width)
    gain_shape = norm_gain.shape
    local = pltpu.with_memory_space_constraint(
        video.reshape(frames, columns, width), pltpu.HBM
    )
    weights = tuple(
        pltpu.with_memory_space_constraint(w, pltpu.HBM)
        for w in (norm_gain, qkv_weight, out_weight)
    )

    sent = call(
        functools.partial(first_kernel, 0),
        [message] * n,
        [HBM] * 4,
        [
            pltpu.VMEM(win_shape, bf16),
            pltpu.VMEM(wout_shape, bf16),
            pltpu.VMEM((2 * width // LANES, tokens // 2, LANES), f32),
            pltpu.VMEM((width // LANES, tokens, LANES), f32),
            pltpu.VMEM((tokens, 3 * width), bf16),
            pltpu.VMEM((tokens, width), bf16),
            pltpu.SemaphoreType.DMA((5,)),
            pltpu.VMEM((2, frames, columns // 2, width), bf16),
            pltpu.VMEM(gain_shape, f32),
        ],
        limit=24,
    )(local, *weights)

    came = {0: sent[0]}
    for k in range(1, n):
        came[k] = lax.ppermute(sent[k], "aa", [(i, i ^ k) for i in range(n)])

    later = range(1, norm_gain.shape[0])
    gain, *fetched = call(
        functools.partial(weights_kernel, later),
        [array(gain_shape, f32)] + [array(win_shape, bf16), array(wout_shape, bf16)] * len(later),
        [HBM] * 3,
        [pltpu.SemaphoreType.DMA((1 + 2 * len(later),))],
    )(*weights)
    win, wout, next_win, next_wout = fetched

    *groups, final = arrival_groups(n)
    ready = []
    for group in groups:
        ready += call(
            functools.partial(group_kernel, 1, len(group)),
            [array((len(group) * per, 3 * width), bf16)],
            [VMEM] * (len(group) + 2),
            [],
        )(*[came[k] for k in group], gain, win)

    lead, *others = (row for rows in row_plan(n) for row in rows)

    def kept(count):
        return array((count, piece, columns, width), bf16)

    mixed, keep, give = call(
        functools.partial(middle_kernel, 1, (*groups, final), lead),
        [array((tokens, width), bf16), kept(1), kept(1)],
        [VMEM] * (n + len(ready) + 3),
        [pltpu.VMEM((len(final) * per, 3 * width), bf16)],
    )(*[came[k] for k in range(n)], *ready, gain, win, wout)

    arrived, starts = [], []

    def swap(value):
        return lax.ppermute(value, "ba", [(0, 1), (1, 0)])

    def project_kept(value):
        count = value.shape[0]
        (packed,) = call(
            functools.partial(kept_kernel, 2),
            [array((count * per, 3 * width), bf16)],
            [VMEM] * 3,
            [],
        )(value, gain, next_win)
        return packed

    def finish(rows, pairs_of_rows, value, other, packed):
        results = call(
            functools.partial(last_kernel, 2, rows),
            [message] * (2 * len(rows)),
            [VMEM] * 6,
            [
                pltpu.VMEM((len(rows) * per, 3 * width), bf16),
                pltpu.VMEM((len(rows) * 2 * per, width), bf16),
            ],
        )(value, other, packed, gain, next_win, next_wout)
        for index, row in enumerate(pairs_of_rows):
            for flip in range(2):
                route = [
                    (2 * a + b, 2 * (a ^ (2 * row + b)) + (b ^ flip))
                    for a in range(n)
                    for b in range(2)
                ]
                arrived.append(lax.ppermute(results[2 * index + flip], ("aa", "ba"), route))
                starts.append((row, flip))

    got = swap(give)
    finish([0], [lead], keep, got, project_kept(keep))

    keep, give = call(
        functools.partial(middle_rest_kernel, others),
        [kept(len(others)), kept(len(others))],
        [VMEM] * (2 + 2 * len(others)),
        [],
    )(
        mixed,
        wout,
        *[came[2 * pair + each] for pair in others for each in range(2)],
    )
    got = swap(give)
    packed = project_kept(keep)
    for rows in row_plan(n)[1:]:
        finish([others.index(row) for row in rows], rows, keep, got, packed)

    def join(values, senders, base=None):
        count = len(values)
        given = [] if base is None else [base]
        return pl.pallas_call(
            functools.partial(join_kernel, senders),
            out_shape=array((frames, columns, width), bf16),
            in_specs=[VMEM] * count + [HBM] * len(given),
            out_specs=HBM,
            scratch_shapes=[pltpu.SemaphoreType.DMA((count,))],
            input_output_aliases={count: 0} if given else {},
            name="join",
            compiler_params=pltpu.CompilerParams(vmem_limit_bytes=4 << 20),
        )(*values, *given)

    slow = [index for index, (row, _) in enumerate(starts) if row == others[0]]
    soon = [index for index in range(n) if index not in slow]
    out = join([arrived[index] for index in soon], [starts[index] for index in soon])
    out = join([arrived[index] for index in slow], [starts[index] for index in slow], out)
    return out.reshape(video.shape)


def body(n, cores, video, norm_gain, qkv_weight, out_weight):
    frames, rows, columns, width = video.shape
    piece = frames // n
    fast = (
        cores == 2
        and rows == 1
        and n % 4 == 0
        and n & (n - 1) == 0
        and LANES % n == 0
        and (LANES // n) % 16 == 0
        and frames % n == 0
        and LANES % frames == 0
        and frames % 8 == 0
        and columns % 16 == 0
        and LANES % (2 * columns) == 0
        and (columns * piece) % LANES == 0
        and (frames * columns) % 256 == 0
        and width == HEADS * HEAD_DIM
        and width % LANES == 0
    )
    if fast:
        return fast_body(n, video, norm_gain, qkv_weight, out_weight)
    return general_body(video, norm_gain, qkv_weight, out_weight)


def row_plan(n):
    half = n // 4
    return [[2 * half - 1], [*range(2 * half - 2, half - 1, -1), *range(half - 1, 0, -1)], [0]]


def arrival_groups(n):
    half, quarter = n // 2, n // 4
    return [
        [0, 1, *range(half, half + quarter)],
        [*range(2, half)],
        [*range(half + quarter, n - 1)],
        [n - 1],
    ]


def solution(mesh):
    n = mesh.shape["aa"]
    return jax.shard_map(
        functools.partial(body, n, mesh.shape["ba"]),
        mesh=mesh,
        in_specs=(P("groups", "aa", "ba", None), P(), P(), P()),
        out_specs=P("groups", "aa", "ba", None),
        check_vma=False,
    )
```
